32 devices in a mesh: row: 8 (over y, x, core), col: 4 (over z).
Axes of the slice: x: 2, y: 2, z: 4, core: 2. Of those that a mesh axis runs over, the one named last changes fastest.
Arguments:
- inverse_blocks: bfloat16 [8, 384, 256, 256], P('row', 'col'), may hold values from -6 to 6
- inverse_rows: int32 [8, 384], P('row', 'col'), may hold values from 0 to 95, as said below
- inverse_cols: int32 [8, 384], P('row', 'col'), may hold values from 0 to 95, as said below
- inverse_count: int32 [8, 4], P('row', 'col'), may hold values from 1 to 96, as said below
- panel_rows: int32 [16], replicated, may hold values from -1 to 95, as said below
- lower_old: bfloat16 [3, 16, 256, 256], P(None, 'row'), may hold values from -0.038085938 to 0.038085938
- lower_new: bfloat16 [3, 3, 256, 256], replicated, may hold values from -0.375 to 0.375
- diag_inverse: float32 [3, 256, 256], replicated, may hold values from -6 to 6
Outputs:
- panel_inverse: bfloat16 [3, 16, 256, 256], P(None, 'row', 'col')
- supernode_inverse: float32 [3, 3, 256, 256], replicated
The draws below stay inside these ranges and needn't reach their ends.
Inputs may be any that keep to these rules, and one draw needn't show every extreme that they name: `panel_rows`: for each row index r in order, 2 entries: distinct block rows congruent to r modulo the number of row indices, at least one, then -1 in the empty slots; some row index fills all 2 in every draw. `inverse_rows`: on row index r every slot names one of the panel rows of r, padding slots too. `inverse_cols`: on column index c every slot names a block column congruent to c modulo the number of column indices; positions may repeat, and repeated blocks add. `inverse_count`: slots 0 to count - 1 of a device's lists are live, the rest padding; one device reaches 96 in every draw.
All inputs are finite; a program needn't handle non-finite values.
Results may differ from the reference program's by a relative error of at most 0.0045.
Values may be sent and summed in bfloat16 or wider, within the bound.
No kernel may reach another device: no remote copies, remote signals or barrier semaphores. Data moves between devices by JAX's collectives and lax.ppermute only.
A program may use at most 128 MiB of HBM per device.

```python
import jax
import jax.numpy as jnp
from jax import lax

B = 256
OLDB = 96
NSUP = 3
SLOTS = 2
KMAX = 96
ROW_GROUPS = 8
COL_GROUPS = 4
STORED = 384
ROWSLOTS = 16
N_COL = 4


def panel_pattern(key):
    base_key = jax.random.fold_in(key, 11)
    first_key, second_key, third_key = jax.random.split(base_key, 3)
    options = (OLDB + ROW_GROUPS - 1) // ROW_GROUPS
    device = jnp.arange(ROW_GROUPS, dtype=jnp.int32)[:, None]
    candidate = jnp.arange(options, dtype=jnp.int32)[None, :]
    scores = jax.random.randint(first_key, (ROW_GROUPS, options), 0, 1 << 20) * options + candidate
    usable = device + ROW_GROUPS * candidate < OLDB
    scores = jnp.where(usable, scores, (1 << 20) * options + candidate)
    ranking = jnp.argsort(scores, axis=1, stable=True)[:, :SLOTS].astype(jnp.int32)
    picked_rows = device + ROW_GROUPS * ranking
    counts = jax.random.randint(second_key, (ROW_GROUPS,), 1, SLOTS + 1)
    fullest = jax.random.randint(third_key, (), 0, ROW_GROUPS)
    counts = jnp.where(jnp.arange(ROW_GROUPS) == fullest, SLOTS, counts)
    pattern_rows = jnp.where(jnp.arange(SLOTS)[None, :] < counts[:, None], picked_rows, -1)
    return (pattern_rows.astype(jnp.int32), counts.astype(jnp.int32))


def draw_panel_rows(key, part):
    pattern_rows, counts = panel_pattern(key)
    return pattern_rows.reshape(-1)


def draw_inverse_rows(key, part):
    pattern_rows, counts = panel_pattern(key)
    picks = jax.random.randint(jax.random.fold_in(key, 23), (ROW_GROUPS, STORED), 0, 1 << 20) % counts[:, None]
    return jnp.take_along_axis(pattern_rows, picks, axis=1).astype(jnp.int32)


def draw_inverse_cols(key, part):
    column = jnp.arange(COL_GROUPS, dtype=jnp.int32)[None, :, None]
    options = (OLDB - column + COL_GROUPS - 1) // COL_GROUPS
    drawn = jax.random.randint(jax.random.fold_in(key, 29), (ROW_GROUPS, COL_GROUPS, KMAX), 0, 1 << 20) % options
    return (column + COL_GROUPS * drawn).reshape(ROW_GROUPS, STORED).astype(jnp.int32)


def draw_inverse_count(key, part):
    first_key, second_key, third_key = jax.random.split(jax.random.fold_in(key, 31), 3)
    first_draw = jax.random.randint(first_key, (ROW_GROUPS * COL_GROUPS,), 1, KMAX + 1)
    second_draw = jax.random.randint(second_key, (ROW_GROUPS * COL_GROUPS,), 1, KMAX + 1)
    counts = jnp.minimum(first_draw, second_draw)
    fullest = jax.random.randint(third_key, (), 0, ROW_GROUPS * COL_GROUPS)
    counts = jnp.where(jnp.arange(ROW_GROUPS * COL_GROUPS) == fullest, KMAX, counts)
    return counts.reshape(ROW_GROUPS, COL_GROUPS).astype(jnp.int32)


def level_of(key, extent, shards, least, high):
    def one(dim, shards_of):
        heights = jax.random.uniform(jax.random.fold_in(jax.random.fold_in(key, 6), dim), (shards_of,), jnp.float32, least / len(shards), high / len(shards))
        return jnp.repeat(jnp.exp(heights), extent[dim] // shards_of).reshape((-1,) + (1,) * (len(extent) - dim - 1))

    factor_of = one(*shards[0])
    for cut in shards[1:]:
        factor_of = factor_of * one(*cut)
    return factor_of


def normal_values(key, extent, width, bound, pieces=(), kind=jnp.bfloat16):
    values = width * jax.random.normal(key, extent, jnp.float32)
    if pieces:
        values = values * level_of(key, extent, pieces, -0.22, 0.18)
    return jnp.clip(values, -bound, bound).astype(kind)


def setup_inputs(seed: int = 0) -> dict:
    key_list = jax.random.split(jax.random.key(seed), 9)
    inverse_blocks = normal_values(key_list[0], (ROW_GROUPS, STORED, B, B), 1.0, 6.0, ((0, 8), (1, 4)))
    inverse_rows = draw_inverse_rows(jax.random.fold_in(key_list[8], 71), 0)
    inverse_cols = draw_inverse_cols(jax.random.fold_in(key_list[8], 71), 0)
    inverse_count = draw_inverse_count(jax.random.fold_in(key_list[8], 71), 0)
    panel_rows = draw_panel_rows(jax.random.fold_in(key_list[8], 71), 0)
    lower_old = normal_values(key_list[5], (NSUP, ROWSLOTS, B, B), (1.0 / (B * KMAX) ** 0.5), 0.038085938, ((1, 8),))
    lower_new = normal_values(key_list[6], (NSUP, NSUP, B, B), B ** -0.5, 0.375)
    diag_inverse = normal_values(key_list[7], (NSUP, B, B), 1.0, 6.0, (), jnp.float32)
    return dict(inverse_blocks=inverse_blocks, inverse_rows=inverse_rows, inverse_cols=inverse_cols, inverse_count=inverse_count, panel_rows=panel_rows, lower_old=lower_old, lower_new=lower_new, diag_inverse=diag_inverse)


exact_mode = lax.Precision.HIGHEST


def linked(blocks_new, left_node, right_node):
    if left_node == right_node:
        return blocks_new[(left_node, left_node)]
    if right_node > left_node:
        return blocks_new[(right_node, left_node)]
    return blocks_new[(left_node, right_node)].T


def reference(inverse_blocks, inverse_rows, inverse_cols, inverse_count, panel_rows, lower_old, lower_new, diag_inverse):
    block_width = inverse_blocks.shape[-1]
    supernodes = lower_old.shape[0]
    live_panel = panel_rows >= 0
    placement = jnp.where(live_panel, panel_rows, OLDB).astype(jnp.int32)
    member = jnp.zeros((OLDB + 1,), jnp.float32).at[placement].max(live_panel.astype(jnp.float32))
    masked = lower_old.astype(jnp.float32) * live_panel.astype(jnp.float32)[None, :, None, None]
    lower_dense = jnp.zeros((supernodes, OLDB + 1, block_width, block_width), jnp.float32).at[:, placement].add(masked)
    entries = inverse_rows.size
    slot_index = jnp.arange(entries, dtype=jnp.int32)
    flat_rows = inverse_rows.reshape(-1).astype(jnp.int32)
    flat_cols = inverse_cols.reshape(-1).astype(jnp.int32)
    device_row = slot_index // (N_COL * KMAX)
    device_col = (slot_index // KMAX) % N_COL
    within = slot_index % KMAX
    is_live = within < inverse_count[device_row, device_col]
    useful = is_live & (member[flat_rows] > 0) & (member[flat_cols] > 0)
    ordering = jnp.argsort(jnp.where(useful, 0, 1).astype(jnp.int32), stable=True).astype(jnp.int32)
    used_count = jnp.sum(useful.astype(jnp.int32))
    flat_blocks = inverse_blocks.reshape(entries, block_width, block_width)

    def accumulate(group_index, running):
        selected = lax.dynamic_slice_in_dim(ordering, group_index * 8, 8)
        is_valid = (group_index * 8 + jnp.arange(8, dtype=jnp.int32)) < used_count
        chosen = flat_blocks[selected].astype(jnp.float32)
        factors = lower_dense[:, flat_cols[selected]]
        products = jnp.einsum("kab,skbc->skac", chosen, factors, precision=exact_mode)
        products = products * is_valid.astype(jnp.float32)[None, :, None, None]
        return running.at[:, flat_rows[selected]].add(products)

    partial_value = lax.fori_loop(0, (used_count + 7) // 8, accumulate,
                            jnp.zeros((supernodes, OLDB + 1, block_width, block_width), jnp.float32))
    lower_links = lower_new.astype(jnp.float32)
    panels = []
    blocks_new = {}
    for node in range(supernodes):
        running = partial_value[node]
        for earlier in range(node):
            running = running + jnp.einsum("nab,bc->nac", panels[earlier].astype(jnp.float32), lower_links[node, earlier], precision=exact_mode)
        current = (-running * member[:, None, None]).astype(jnp.bfloat16)
        current_wide = current.astype(jnp.float32)
        for earlier in range(node):
            crossed = jnp.einsum("nab,nac->bc", panels[earlier].astype(jnp.float32), lower_dense[node], precision=exact_mode)
            for another in range(node):
                crossed = crossed + jnp.dot(linked(blocks_new, earlier, another), lower_links[node, another], precision=exact_mode)
            blocks_new[(node, earlier)] = -crossed
        diagonal_block = diag_inverse[node] - jnp.einsum("nab,nac->bc", lower_dense[node], current_wide, precision=exact_mode)
        for earlier in range(node):
            diagonal_block = diagonal_block - jnp.dot(lower_links[node, earlier].T, blocks_new[(node, earlier)], precision=exact_mode)
        blocks_new[(node, node)] = diagonal_block
        panels.append(current)
    panel_inverse = jnp.stack([panel[placement] for panel in panels])
    empty_block = jnp.zeros((block_width, block_width), jnp.float32)
    supernode_inverse = jnp.stack([
        jnp.stack([blocks_new[(node, earlier)] if earlier <= node else empty_block for earlier in range(supernodes)])
        for node in range(supernodes)])
    return panel_inverse, supernode_inverse
```

```python
import functools

import jax
import jax.numpy as jnp
from jax import lax
from jax.experimental import pallas as pl
from jax.experimental.pallas import tpu as pltpu
from jax.sharding import PartitionSpec as P


BF16 = jnp.bfloat16
F32 = jnp.float32
VMEM = pl.BlockSpec(memory_space=pltpu.VMEM)
ANY = pl.BlockSpec(memory_space=pl.ANY)
SMEM = pl.BlockSpec(memory_space=pltpu.SMEM)
DEPTH = 8


def permute(value, pairs):
    return lax.ppermute(value, ("row", "col"), pairs)


def gather_kernel(n_cand, code, blocks, w_hi, w_lo, acc, order, buf, sem):
    kmax = code.shape[0]
    width = buf.shape[-1]

    def scan(k, n):
        order[n] = k
        return n + (code[k] >= 0).astype(jnp.int32)

    n_used = lax.fori_loop(0, kmax, scan, jnp.int32(0))

    def fetch(i):
        slot = lax.rem(i, DEPTH)
        return pltpu.make_async_copy(blocks.at[order[i]], buf.at[slot], sem.at[slot])

    for i in range(DEPTH):

        @pl.when(i < n_used)
        def _():
            fetch(jnp.int32(i)).start()

    acc[...] = jnp.zeros_like(acc)

    def step(i, carry):
        fetch(i).wait()
        target = code[order[i]]
        slot = lax.rem(i, DEPTH)
        acc[target] += buf[slot].astype(F32)

        @pl.when(i + DEPTH < n_used)
        def _():
            fetch(i + DEPTH).start()

        return carry

    lax.fori_loop(0, n_used, step, 0)
    for index in range(acc.shape[0]):
        s, p = divmod(index, n_cand)
        rows = pl.ds(s * width, width)
        cols = pl.ds(p * width, width)
        value = acc[index]
        high = value.astype(BF16)
        w_hi[rows, cols] = high
        w_lo[rows, cols] = (value - high.astype(F32)).astype(BF16)


def main_kernel(n_parts, n_col, where, w_hi, w_lo, old, new, *refs):
    t_count = new.shape[0]
    mine = refs[: n_parts * t_count]
    theirs = refs[n_parts * t_count : 2 * n_parts * t_count]
    rest = refs[2 * n_parts * t_count :]
    u_own = rest[0]
    u_send = rest[1:n_col]
    g_keep, g_send = rest[n_col : n_col + 2]
    lo, u_all, g_all, sems = rest[n_col + 2 :]
    width = new.shape[-1]
    slots = old.shape[1]
    part_rows = slots * width

    def copies(group, t):
        return [
            pltpu.make_async_copy(
                group[t * n_parts + m], lo.at[t, pl.ds(m * part_rows, part_rows), :], sems.at[t, m]
            )
            for m in range(n_parts)
        ]

    for t in range(t_count):

        @pl.when(where[0] == 1)
        def _():
            for copy in copies(mine, t):
                copy.start()

        @pl.when(where[0] == 0)
        def _():
            for copy in copies(theirs, t):
                copy.start()

    panels = []
    index = 0
    for t in range(t_count):
        for copy in copies(mine, t):
            copy.wait()
        lo_t = lo[t]
        running = jnp.dot(w_hi[...], lo_t, preferred_element_type=F32)
        running += jnp.dot(w_lo[...], lo_t, preferred_element_type=F32)
        for s in range(t):
            running += jnp.dot(panels[s], new[t, s], preferred_element_type=F32)
        current = -running
        u_all[t] = current
        panels.append(current.astype(BF16))
        own = old[t].reshape(part_rows, width)
        for s in range(t + 1):
            left, right = (own, panels[t]) if s == t else (panels[s], own)
            g_all[pl.ds(index * width, width), :] = lax.dot_general(
                left, right, (((0,), (0,)), ((), ())), preferred_element_type=F32
            )
            index += 1
    half = g_keep.shape[0]
    g_keep[...] = g_all[pl.ds(pl.multiple_of(where[1] * half, 16), half), :]
    g_send[...] = g_all[pl.ds(pl.multiple_of((1 - where[1]) * half, 16), half), :].astype(BF16)
    share = width // n_col
    for t in range(t_count):
        for s in range(slots):
            for m in range(n_col):
                start = s * width + (where[2] ^ m) * share
                value = u_all[t, pl.ds(pl.multiple_of(start, 16), share), :]
                if m == 0:
                    u_own[t, s] = value
                else:
                    u_send[m - 1][t, s] = value.astype(BF16)


def split_kernel(where, keep, received, own, *sends):
    rows = own.shape[0]

    def piece(m):
        window = pl.ds(pl.multiple_of((where[3] ^ m) * rows, 16), rows)
        return keep[window, :] + received[window, :].astype(F32)

    own[...] = piece(0)
    for m, send in enumerate(sends):
        send[...] = piece(m + 1).astype(BF16)


def tree(values):
    while len(values) > 1:
        values = [a + b for a, b in zip(values[::2], values[1::2])]
    return values[0]


def add_kernel(*refs):
    out = refs[-1]
    out[...] = tree([ref[...].astype(F32) for ref in refs[:-1]]).astype(out.dtype)


def wide_dot(left, right, dims):
    dims = (dims, ((), ()))
    if left.dtype == F32:
        high = left.astype(BF16)
        low = (left - high.astype(F32)).astype(BF16)
        return lax.dot_general(high, right, dims, preferred_element_type=F32) + lax.dot_general(
            low, right, dims, preferred_element_type=F32
        )
    high = right.astype(BF16)
    low = (right - high.astype(F32)).astype(BF16)
    return lax.dot_general(left, high, dims, preferred_element_type=F32) + lax.dot_general(
        left, low, dims, preferred_element_type=F32
    )


def final_kernel(n_plane, where, new, diag, *refs):
    pieces = refs[: 2 * n_plane]
    out, g_all = refs[2 * n_plane :]
    t_count = new.shape[0]
    width = new.shape[-1]
    rows = pieces[0].shape[0]
    for index, piece in enumerate(pieces):
        h, m = divmod(index, n_plane)
        place = (where[1] ^ h) * n_plane + (where[3] ^ m)
        g_all[pl.ds(pl.multiple_of(place * rows, 16), rows), :] = piece[...]

    def g(t, s):
        index = t * (t + 1) // 2 + s
        return g_all[pl.ds(index * width, width), :].astype(F32)

    blocks = {}
    for t in range(t_count):
        for s in range(t):
            crossed = g(t, s)
            for u in range(t):
                if u >= s:
                    crossed += wide_dot(blocks[u, s], new[t, u], ((1,), (0,)))
                else:
                    crossed += wide_dot(blocks[s, u], new[t, u], ((0,), (0,)))
            blocks[t, s] = -crossed
            out[t, s] = blocks[t, s]
        diagonal = diag[t] - g(t, t)
        for s in range(t):
            diagonal -= wide_dot(new[t, s], blocks[t, s], ((0,), (0,)))
        blocks[t, t] = diagonal
        out[t, t] = diagonal
        for s in range(t + 1, t_count):
            out[t, s] = jnp.zeros((width, width), F32)


def call(kernel, shapes, in_specs, scratch=(), flops=0, moved=0, limit=8):
    return pl.pallas_call(
        kernel,
        out_shape=shapes,
        in_specs=in_specs,
        out_specs=jax.tree.map(lambda _: VMEM, shapes),
        scratch_shapes=list(scratch),
        cost_estimate=pl.CostEstimate(flops=flops, bytes_accessed=moved, transcendentals=0),
        compiler_params=pltpu.CompilerParams(vmem_limit_bytes=limit << 20),
    )


def per_device(
    inverse_blocks,
    inverse_rows,
    inverse_cols,
    inverse_count,
    panel_rows,
    lower_old,
    lower_new,
    diag_inverse,
):
    blocks = inverse_blocks[0]
    stored_rows = inverse_rows[0]
    stored_cols = inverse_cols[0]
    stored_count = inverse_count[0, 0]
    kmax = blocks.shape[0]
    width = blocks.shape[-1]
    t_count, slots = lower_old.shape[:2]
    n_row = lax.axis_size("row")
    n_col = lax.axis_size("col")
    row_me = lax.axis_index("row")
    col_me = lax.axis_index("col")
    devices = [(r, c) for r in range(n_row) for c in range(n_col)]
    n_high = n_row // n_col
    n_plane = n_row // 2

    def pairs(active, partner):
        return [
            (r * n_col + c, pr * n_col + pc)
            for r, c in devices
            if active(r, c)
            for pr, pc in [partner(r, c)]
        ]

    high_me = row_me // n_col
    own_rows = lax.dynamic_slice_in_dim(panel_rows, row_me * slots, slots)
    groups = (jnp.arange(n_high, dtype=jnp.int32) ^ high_me) * n_col + col_me
    cand_rows = panel_rows.reshape(n_row, slots)[groups].reshape(-1)
    n_cand = n_high * slots
    at_row = stored_rows[:, None] == own_rows[None, :]
    at_cand = stored_cols[:, None] == cand_rows[None, :]
    live = jnp.arange(kmax, dtype=jnp.int32) < stored_count
    useful = live & jnp.any(at_row, axis=1) & jnp.any(at_cand, axis=1)
    slot_of = jnp.sum(jnp.where(at_row, jnp.arange(slots, dtype=jnp.int32), 0), axis=1)
    cand_of = jnp.sum(jnp.where(at_cand, jnp.arange(n_cand, dtype=jnp.int32), 0), axis=1)
    code = jnp.where(useful, slot_of * n_cand + cand_of, -1).astype(jnp.int32)
    source = ((row_me ^ col_me) & 1 == 0).astype(jnp.int32)
    where = jnp.stack([source, row_me & 1, col_me, row_me >> 1]).astype(jnp.int32)

    same_core = lambda r, c: (r ^ c) & 1 == 0
    parts = {}
    for t in range(t_count):
        hold = lower_old[t].reshape(slots * width, width)
        bit = n_col // 2
        while bit >= 2:
            mask = 2 * bit - 1
            received = permute(
                hold,
                pairs(lambda r, c: (r ^ c) & mask == 0, lambda r, c: (r ^ bit, c)),
            )
            hold = jnp.where((row_me ^ col_me) & bit == 0, hold, received)
            bit //= 2
        held = [hold]
        bit = n_col
        while bit < n_row:
            held += [permute(h, pairs(same_core, lambda r, c: (r ^ bit, c))) for h in held]
            bit *= 2
        for m, h in enumerate(held):
            parts[t, m] = (h, permute(h, pairs(same_core, lambda r, c: (r ^ 1, c))))

    block = width * width
    w_shape = jax.ShapeDtypeStruct((slots * width, n_cand * width), BF16)
    w_hi, w_lo = call(
        functools.partial(gather_kernel, n_cand),
        (w_shape, w_shape),
        [SMEM, ANY],
        [
            pltpu.VMEM((slots * n_cand, width, width), F32),
            pltpu.SMEM((kmax,), jnp.int32),
            pltpu.VMEM((DEPTH, width, width), BF16),
            pltpu.SemaphoreType.DMA((DEPTH,)),
        ],
        flops=block * 16,
        moved=16 * block * 2 + 16 * n_cand * slots * block,
        limit=54,
    )(code, blocks)

    order = [(t, m) for t in range(t_count) for m in range(n_high)]
    share = width // n_col
    n_blocks = t_count * (t_count + 1) // 2
    half = n_blocks * width // 2
    piece = half // n_plane
    u_shape = (t_count, slots, share, width)
    outs = call(
        functools.partial(main_kernel, n_high, n_col),
        (
            jax.ShapeDtypeStruct(u_shape, F32),
            *[jax.ShapeDtypeStruct(u_shape, BF16)] * (n_col - 1),
            jax.ShapeDtypeStruct((half, width), F32),
            jax.ShapeDtypeStruct((half, width), BF16),
        ),
        [SMEM, VMEM, VMEM, VMEM, VMEM] + [ANY] * (2 * len(order)),
        [
            pltpu.VMEM((t_count, n_cand * width, width), BF16),
            pltpu.VMEM((t_count, slots * width, width), F32),
            pltpu.VMEM((n_blocks * width, width), F32),
            pltpu.SemaphoreType.DMA((t_count, n_high)),
        ],
        flops=2 * block * width * slots * t_count * (2 * n_cand + 4),
        moved=4 * block * t_count * n_cand,
        limit=16 + (2 * t_count * n_cand * block + 4 * slots * n_cand * block) // 2**20,
    )(
        where,
        w_hi,
        w_lo,
        lower_old,
        lower_new,
        *[parts[key][0] for key in order],
        *[parts[key][1] for key in order],
    )
    u_own, u_sends, g_keep, g_send = outs[0], outs[1:n_col], outs[n_col], outs[n_col + 1]

    anyone = lambda r, c: True
    g_received = permute(g_send, pairs(anyone, lambda r, c: (r ^ 1, c)))
    own, *sends = call(
        split_kernel,
        (
            jax.ShapeDtypeStruct((piece, width), F32),
            *[jax.ShapeDtypeStruct((piece, width), BF16)] * (n_plane - 1),
        ),
        [SMEM, VMEM, VMEM],
        flops=half * width,
        moved=half * width * 8,
    )(where, g_keep, g_received)
    arrived = [
        permute(send, pairs(anyone, lambda r, c: (r ^ 2 * (m + 1), c)))
        for m, send in enumerate(sends)
    ]

    def add(values):
        shape = values[0].shape
        return call(
            add_kernel,
            jax.ShapeDtypeStruct(shape, BF16),
            [VMEM] * len(values),
            flops=len(values) * values[0].size,
            moved=values[0].size * 2 * len(values),
        )(*values)

    in_plane = add([own, *arrived])
    level = [in_plane] + [
        permute(in_plane, pairs(anyone, lambda r, c: (r, c ^ m))) for m in range(1, n_col)
    ]
    total = add(level)
    u_arrived = [
        permute(u_sends[m - 1], pairs(anyone, lambda r, c: (r, c ^ m))) for m in range(1, n_col)
    ]
    plane = [total] + [
        permute(total, pairs(anyone, lambda r, c: (r ^ 2 * m, c))) for m in range(1, n_plane)
    ]
    other = [permute(value, pairs(anyone, lambda r, c: (r ^ 1, c))) for value in plane]
    supernode_inverse = call(
        functools.partial(final_kernel, n_plane),
        jax.ShapeDtypeStruct((t_count, t_count, width, width), F32),
        [SMEM] + [VMEM] * (2 + 2 * n_plane),
        [pltpu.VMEM((n_blocks * width, width), BF16)],
        flops=2 * block * width * 16,
        moved=block * t_count * t_count * 6,
    )(where, lower_new, diag_inverse, *plane, *other)
    panel_inverse = add([u_own, *u_arrived])
    return (panel_inverse, supernode_inverse)


def solution(mesh):
    placed = (
        P("row", "col", None, None),
        P("row", "col"),
        P("row", "col"),
        P("row", "col"),
        P(),
        P(None, "row", None, None),
        P(),
        P(),
    )
    return jax.shard_map(
        per_device,
        mesh=mesh,
        in_specs=placed,
        out_specs=(P(None, "row", "col", None), P()),
        check_vma=False,
    )
```

```python
import functools

import jax
import jax.numpy as jnp
from jax import lax
from jax.experimental import pallas as pl
from jax.experimental.pallas import tpu as pltpu
from jax.sharding import PartitionSpec as P


BF16 = jnp.bfloat16
F32 = jnp.float32
VMEM = pl.BlockSpec(memory_space=pltpu.VMEM)
ANY = pl.BlockSpec(memory_space=pl.ANY)
SMEM = pl.BlockSpec(memory_space=pltpu.SMEM)
DEPTH = 8


def permute(value, pairs):
    return lax.ppermute(value, ("row", "col"), pairs)


def gather_kernel(
    groups, slots, me, rows_ref, cols_ref, count, panel, blocks, w_out, *refs
):
    marks = refs[:groups]
    acc, w, order, code, buf, sem, out_sem = refs[groups:]
    width = buf.shape[-1]
    n_cand = groups * slots
    row_me = me[0]
    for mark in marks:
        mark[0] = me[1 + groups]
    own = [panel[row_me * slots + s] for s in range(slots)]
    cand = [panel[me[1 + g] * slots + s] for g in range(groups) for s in range(slots)]

    def scan(k, n):
        row, col = rows_ref[0, k], cols_ref[0, k]
        where = jnp.int32(-1)
        for p in range(n_cand):
            where = jnp.where(col == cand[p], p, where)
        slot = jnp.int32(-1)
        for s in range(slots):
            slot = jnp.where(row == own[s], s, slot)
        order[n] = k
        code[n] = slot * n_cand + where
        return n + ((where >= 0) & (slot >= 0)).astype(jnp.int32)

    n_used = lax.fori_loop(0, count[0, 0], scan, jnp.int32(0))

    def fetch(i):
        slot = lax.rem(i, DEPTH)
        return pltpu.make_async_copy(blocks.at[order[i]], buf.at[slot], sem.at[slot])

    for i in range(DEPTH):

        @pl.when(i < n_used)
        def _():
            fetch(jnp.int32(i)).start()

    acc[...] = jnp.zeros_like(acc)

    def step(i, carry):
        fetch(i).wait()
        target = code[i]
        slot = lax.rem(i, DEPTH)
        acc[target] += buf[slot].astype(F32)

        @pl.when(i + DEPTH < n_used)
        def _():
            fetch(i + DEPTH).start()

        return carry

    lax.fori_loop(0, n_used, step, 0)
    for index in range(acc.shape[0]):
        s, p = divmod(index, n_cand)
        rows = pl.ds(s * width, width)
        cols = pl.ds(p * width, width)
        value = acc[index]
        high = value.astype(BF16)
        w[0, rows, cols] = high
        w[1, rows, cols] = (value - high.astype(F32)).astype(BF16)
    copy = pltpu.make_async_copy(w, w_out, out_sem)
    copy.start()
    copy.wait()


def main_kernel(n_high, n_col, where, w_in, old, new, *refs):
    t_count = new.shape[0]
    mine = refs[:n_high]
    theirs = refs[n_high : 2 * n_high]
    rest = refs[2 * n_high :]
    u_own = rest[0]
    u_send = rest[1:n_col]
    g_keep, g_send = rest[n_col : n_col + 2]
    w, lo, u_all, g_all, w_sem, sems = rest[n_col + 2 :]
    width = new.shape[-1]
    slots = old.shape[1]
    part_rows = slots * width
    w_copy = pltpu.make_async_copy(w_in, w, w_sem)
    w_copy.start()

    def copies(group, t):
        return [
            pltpu.make_async_copy(
                group[m].at[t, s],
                lo.at[t, pl.ds((m * slots + s) * width, width), :],
                sems.at[t, m * slots + s],
            )
            for m in range(n_high)
            for s in range(slots)
        ]

    @pl.when(where[0] == 1)
    def _():
        for t in range(t_count):
            for copy in copies(mine, t):
                copy.start()

    @pl.when(where[0] == 0)
    def _():
        for t in range(t_count):
            for copy in copies(theirs, t):
                copy.start()

    w_copy.wait()
    panels = []
    index = 0
    for t in range(t_count):
        for copy in copies(mine, t):
            copy.wait()
        lo_t = lo[t]
        running = jnp.dot(w[0], lo_t, preferred_element_type=F32)
        running += jnp.dot(w[1], lo_t, preferred_element_type=F32)
        for s in range(t):
            running += jnp.dot(panels[s], new[t, s], preferred_element_type=F32)
        current = -running
        u_all[t] = current
        panels.append(current.astype(BF16))
        own = old[t].reshape(part_rows, width)
        for s in range(t + 1):
            left, right = (own, panels[t]) if s == t else (panels[s], own)
            g_all[pl.ds(index * width, width), :] = lax.dot_general(
                left, right, (((0,), (0,)), ((), ())), preferred_element_type=F32
            )
            index += 1
    half = g_keep.shape[0]
    g_keep[...] = g_all[pl.ds(pl.multiple_of(where[1] * half, 16), half), :]
    g_send[...] = g_all[pl.ds(pl.multiple_of((1 - where[1]) * half, 16), half), :].astype(BF16)
    share = width // n_col
    for t in range(t_count):
        for s in range(slots):
            for m in range(n_col):
                start = s * width + (where[2] ^ m) * share
                value = u_all[t, pl.ds(pl.multiple_of(start, 16), share), :]
                if m == 0:
                    u_own[t, s] = value
                else:
                    u_send[m - 1][t, s] = value.astype(BF16)


def split_kernel(where, keep, received, own, *sends):
    rows = own.shape[0]

    def piece(m):
        window = pl.ds(pl.multiple_of((where[3] ^ m) * rows, 16), rows)
        return keep[window, :] + received[window, :].astype(F32)

    own[...] = piece(0)
    for m, send in enumerate(sends):
        send[...] = piece(m + 1).astype(BF16)


def tree(values):
    while len(values) > 1:
        values = [a + b for a, b in zip(values[::2], values[1::2])]
    return values[0]


def add_kernel(*refs):
    out = refs[-1]
    out[...] = tree([ref[...].astype(F32) for ref in refs[:-1]]).astype(out.dtype)


def wide_dot(left, right, dims):
    dims = (dims, ((), ()))
    if left.dtype == F32:
        high = left.astype(BF16)
        low = (left - high.astype(F32)).astype(BF16)
        return lax.dot_general(high, right, dims, preferred_element_type=F32) + lax.dot_general(
            low, right, dims, preferred_element_type=F32
        )
    high = right.astype(BF16)
    low = (right - high.astype(F32)).astype(BF16)
    return lax.dot_general(left, high, dims, preferred_element_type=F32) + lax.dot_general(
        left, low, dims, preferred_element_type=F32
    )


def final_kernel(n_plane, where, new, diag, *refs):
    pieces = refs[: 2 * n_plane]
    out, g_all = refs[2 * n_plane :]
    t_count = new.shape[0]
    width = new.shape[-1]
    rows = pieces[0].shape[0]
    for index, piece in enumerate(pieces):
        h, m = divmod(index, n_plane)
        place = (where[1] ^ h) * n_plane + (where[3] ^ m)
        g_all[pl.ds(pl.multiple_of(place * rows, 16), rows), :] = piece[...]

    def g(t, s):
        index = t * (t + 1) // 2 + s
        return g_all[pl.ds(index * width, width), :].astype(F32)

    blocks = {}
    for t in range(t_count):
        for s in range(t):
            crossed = g(t, s)
            for u in range(t):
                if u >= s:
                    crossed += wide_dot(blocks[u, s], new[t, u], ((1,), (0,)))
                else:
                    crossed += wide_dot(blocks[s, u], new[t, u], ((0,), (0,)))
            blocks[t, s] = -crossed
            out[t, s] = blocks[t, s]
        diagonal = diag[t] - g(t, t)
        for s in range(t):
            diagonal -= wide_dot(new[t, s], blocks[t, s], ((0,), (0,)))
        blocks[t, t] = diagonal
        out[t, t] = diagonal
        for s in range(t + 1, t_count):
            out[t, s] = jnp.zeros((width, width), F32)


def call(kernel, shapes, in_specs, scratch=(), flops=0, moved=0, limit=8):
    def place(shape):
        if not isinstance(shape, jax.ShapeDtypeStruct):
            return ANY
        return SMEM if shape.dtype == jnp.int32 else VMEM

    return pl.pallas_call(
        kernel,
        out_shape=shapes,
        in_specs=in_specs,
        out_specs=tuple(map(place, shapes)) if isinstance(shapes, tuple) else place(shapes),
        scratch_shapes=list(scratch),
        cost_estimate=pl.CostEstimate(flops=flops, bytes_accessed=moved, transcendentals=0),
        compiler_params=pltpu.CompilerParams(vmem_limit_bytes=limit << 20),
    )


def per_device(
    inverse_blocks,
    inverse_rows,
    inverse_cols,
    inverse_count,
    panel_rows,
    lower_old,
    lower_new,
    diag_inverse,
):
    blocks = inverse_blocks[0]
    stored_rows = inverse_rows[0]
    stored_cols = inverse_cols[0]
    stored_count = inverse_count[0, 0]
    kmax = blocks.shape[0]
    width = blocks.shape[-1]
    t_count, slots = lower_old.shape[:2]
    n_row = lax.axis_size("row")
    n_col = lax.axis_size("col")
    row_me = lax.axis_index("row")
    col_me = lax.axis_index("col")
    devices = [(r, c) for r in range(n_row) for c in range(n_col)]
    n_high = n_row // n_col
    n_plane = n_row // 2

    def pairs(active, partner):
        return [
            (r * n_col + c, pr * n_col + pc)
            for r, c in devices
            if active(r, c)
            for pr, pc in [partner(r, c)]
        ]

    high_me = row_me // n_col
    groups = [((high_me ^ g) * n_col + col_me) for g in range(n_high)]
    n_cand = n_high * slots
    me = jnp.stack([row_me, *groups, row_me ^ col_me]).astype(jnp.int32)
    source = ((row_me ^ col_me) & 1 == 0).astype(jnp.int32)
    where = jnp.stack([source, row_me & 1, col_me, row_me >> 1]).astype(jnp.int32)

    block = width * width
    w_shape = (2, slots * width, n_cand * width)
    w, *marks = call(
        functools.partial(gather_kernel, n_high, slots),
        (
            pltpu.MemorySpace.HBM(w_shape, BF16),
            *[jax.ShapeDtypeStruct((1,), jnp.int32)] * n_high,
        ),
        [SMEM, SMEM, SMEM, SMEM, SMEM, ANY],
        [
            pltpu.VMEM((slots * n_cand, width, width), F32),
            pltpu.VMEM(w_shape, BF16),
            pltpu.SMEM((kmax,), jnp.int32),
            pltpu.SMEM((kmax,), jnp.int32),
            pltpu.VMEM((DEPTH, width, width), BF16),
            pltpu.SemaphoreType.DMA((DEPTH,)),
            pltpu.SemaphoreType.DMA,
        ],
        flops=block * 16,
        moved=16 * block * 2 + 16 * n_cand * slots * block,
        limit=6 + (slots * n_cand * 8 * block + DEPTH * 2 * block) // 2**20,
    )(
        me,
        inverse_rows,
        inverse_cols,
        inverse_count,
        panel_rows,
        pltpu.with_memory_space_constraint(blocks, pltpu.MemorySpace.HBM),
    )

    def spread(group, offset):
        table = {}
        for r, c in devices:
            if r % n_col == c:
                table[r, c] = ((r // n_col ^ group) * n_col + (c ^ offset), c)
        targets = set(table.values())
        for r, c in devices:
            if (r ^ c) & 1 == 0:
                sends, takes = (r, c) in table, (r, c) in targets
                if not sends:
                    table[r, c] = (r ^ 1, c)
                if not takes:
                    table[r ^ 1, c] = (r, c)
        return [(r * n_col + c, pr * n_col + pc) for (r, c), (pr, pc) in table.items()]

    anyone = lambda r, c: True
    keys = [(m, o) for m in range(n_high) for o in reversed(range(0, n_col, 2)) if (m, o) != (0, 0)]
    arrived = {key: permute(lower_old, spread(*key)) for key in keys}
    arrived[0, 0] = lower_old
    parts = []
    for m in range(n_high):
        part = arrived[m, 0]
        for o in range(2, n_col, 2):
            part = jnp.where(marks[m][0] & (n_col - 2) == o, arrived[m, o], part)
        parts.append((part, permute(part, pairs(anyone, lambda r, c: (r ^ 1, c)))))

    share = width // n_col
    n_blocks = t_count * (t_count + 1) // 2
    half = n_blocks * width // 2
    piece = half // n_plane
    u_shape = (t_count, slots, share, width)
    outs = call(
        functools.partial(main_kernel, n_high, n_col),
        (
            jax.ShapeDtypeStruct(u_shape, F32),
            *[jax.ShapeDtypeStruct(u_shape, BF16)] * (n_col - 1),
            jax.ShapeDtypeStruct((half, width), F32),
            jax.ShapeDtypeStruct((half, width), BF16),
        ),
        [SMEM, ANY, VMEM, VMEM] + [ANY] * (2 * n_high),
        [
            pltpu.VMEM(w_shape, BF16),
            pltpu.VMEM((t_count, n_cand * width, width), BF16),
            pltpu.VMEM((t_count, slots * width, width), F32),
            pltpu.VMEM((n_blocks * width, width), F32),
            pltpu.SemaphoreType.DMA,
            pltpu.SemaphoreType.DMA((t_count, n_cand)),
        ],
        flops=2 * block * width * slots * t_count * (2 * n_cand + 4),
        moved=4 * block * t_count * n_cand,
        limit=16 + (2 * t_count * n_cand * block + 4 * slots * n_cand * block) // 2**20,
    )(
        where,
        pltpu.with_memory_space_constraint(w, pltpu.MemorySpace.HBM),
        lower_old,
        lower_new,
        *[part[0] for part in parts],
        *[part[1] for part in parts],
    )
    u_own, u_sends, g_keep, g_send = outs[0], outs[1:n_col], outs[n_col], outs[n_col + 1]

    g_received = permute(g_send, pairs(anyone, lambda r, c: (r ^ 1, c)))
    own, *sends = call(
        split_kernel,
        (
            jax.ShapeDtypeStruct((piece, width), F32),
            *[jax.ShapeDtypeStruct((piece, width), BF16)] * (n_plane - 1),
        ),
        [SMEM, VMEM, VMEM],
        flops=half * width,
        moved=half * width * 8,
    )(where, g_keep, g_received)
    arrived = [
        permute(send, pairs(anyone, lambda r, c: (r ^ 2 * (m + 1), c)))
        for m, send in enumerate(sends)
    ]

    def add(values):
        shape = values[0].shape
        return call(
            add_kernel,
            jax.ShapeDtypeStruct(shape, BF16),
            [VMEM] * len(values),
            flops=len(values) * values[0].size,
            moved=values[0].size * 2 * len(values),
        )(*values)

    in_plane = add([own, *arrived])
    level = [in_plane] + [
        permute(in_plane, pairs(anyone, lambda r, c: (r, c ^ m))) for m in range(1, n_col)
    ]
    total = add(level)
    u_arrived = [
        permute(u_sends[m - 1], pairs(anyone, lambda r, c: (r, c ^ m))) for m in range(1, n_col)
    ]
    plane = [total] + [
        permute(total, pairs(anyone, lambda r, c: (r ^ 2 * m, c))) for m in range(1, n_plane)
    ]
    other = [permute(value, pairs(anyone, lambda r, c: (r ^ 1, c))) for value in plane]
    supernode_inverse = call(
        functools.partial(final_kernel, n_plane),
        jax.ShapeDtypeStruct((t_count, t_count, width, width), F32),
        [SMEM] + [VMEM] * (2 + 2 * n_plane),
        [pltpu.VMEM((n_blocks * width, width), BF16)],
        flops=2 * block * width * 16,
        moved=block * t_count * t_count * 6,
    )(where, lower_new, diag_inverse, *plane, *other)
    panel_inverse = add([u_own, *u_arrived])
    return (panel_inverse, supernode_inverse)


def solution(mesh):
    placed = (
        P("row", "col", None, None),
        P("row", "col"),
        P("row", "col"),
        P("row", "col"),
        P(),
        P(None, "row", None, None),
        P(),
        P(),
    )
    return jax.shard_map(
        per_device,
        mesh=mesh,
        in_specs=placed,
        out_specs=(P(None, "row", "col", None), P()),
        check_vma=False,
    )
```

```python
import functools

import jax
import jax.numpy as jnp
from jax import lax
from jax.experimental import pallas as pl
from jax.experimental.pallas import tpu as pltpu
from jax.sharding import PartitionSpec as P


BF16 = jnp.bfloat16
F32 = jnp.float32
VMEM = pl.BlockSpec(memory_space=pltpu.VMEM)
ANY = pl.BlockSpec(memory_space=pl.ANY)
SMEM = pl.BlockSpec(memory_space=pltpu.SMEM)
DEPTH = 8


def permute(value, pairs):
    return lax.ppermute(value, ("row", "col"), pairs)


def gather_kernel(groups, slots, me, count, rows_in, cols_in, panel_in, blocks, *refs):
    w_outs = refs[:groups]
    acc, w, order, code, buf, rows_ref, cols_ref, panel, sem, out_sem, in_sem = refs[groups:]
    width = buf.shape[-1]
    n_cand = groups * slots
    row_me = me[0]
    tables = ((rows_in, rows_ref), (cols_in, cols_ref), (panel_in, panel))
    brought = [pltpu.make_async_copy(*pair, in_sem.at[i]) for i, pair in enumerate(tables)]
    for copy in brought:
        copy.start()
    acc[...] = jnp.zeros_like(acc)
    for copy in brought:
        copy.wait()
    own = [panel[row_me * slots + s] for s in range(slots)]
    cand = [panel[me[1 + g] * slots + s] for g in range(groups) for s in range(slots)]
    step_size = 8 if rows_ref.shape[1] % 8 == 0 else 1

    def scan(step, n):
        for u in range(step_size):
            k = step * step_size + u
            row, col = rows_ref[0, k], cols_ref[0, k]
            where = jnp.int32(-1)
            for p in range(n_cand):
                where = jnp.where(col == cand[p], p, where)
            slot = jnp.int32(-1)
            for s in range(slots):
                slot = jnp.where(row == own[s], s, slot)
            order[n] = k
            code[n] = slot * n_cand + where
            used = (where >= 0) & (slot >= 0) & (k < count[0, 0])
            n = n + used.astype(jnp.int32)
        return n

    n_steps = (count[0, 0] + step_size - 1) // step_size
    n_used = lax.fori_loop(0, n_steps, scan, jnp.int32(0))

    def fetch(i):
        slot = lax.rem(i, DEPTH)
        return pltpu.make_async_copy(blocks.at[order[i]], buf.at[slot], sem.at[slot])

    for i in range(DEPTH):

        @pl.when(i < n_used)
        def _():
            fetch(jnp.int32(i)).start()

    def step(i, carry):
        fetch(i).wait()
        target = code[i]
        slot = lax.rem(i, DEPTH)
        acc[target] += buf[slot].astype(F32)

        @pl.when(i + DEPTH < n_used)
        def _():
            fetch(i + DEPTH).start()

        return carry

    lax.fori_loop(0, n_used, step, 0)
    for g in range(groups):
        for s in range(slots):
            for p in range(slots):
                rows = pl.ds(s * width, width)
                cols = pl.ds(p * width, width)
                value = acc[s * n_cand + g * slots + p]
                high = value.astype(BF16)
                w[g, 0, rows, cols] = high
                w[g, 1, rows, cols] = (value - high.astype(F32)).astype(BF16)
        pltpu.make_async_copy(w.at[g], w_outs[g], out_sem.at[g]).start()
    for g in range(groups):
        pltpu.make_async_copy(w.at[g], w_outs[g], out_sem.at[g]).wait()


def fill(where, options, lo, sems):
    count, slots, width = options[0].shape[:3]

    def copies(part, t):
        return [
            pltpu.make_async_copy(
                part.at[t, p], lo.at[t, pl.ds(p * width, width), :], sems.at[t, p]
            )
            for p in range(slots)
        ]

    for case, part in enumerate(options):

        @pl.when(where[0] == case)
        def _():
            for t in range(count):
                for copy in copies(part, t):
                    copy.start()

    def wait(t):
        for copy in copies(options[0], t):
            copy.wait()

    return wait


def own_kernel(where, w_in, *refs):
    options, (p_out, w, lo, w_sem, sems) = refs[:-5], refs[-5:]
    w_copy = pltpu.make_async_copy(w_in, w, w_sem)
    w_copy.start()
    wait = fill(where, options, lo, sems)
    w_copy.wait()
    for t in range(lo.shape[0]):
        wait(t)
        lo_t = lo[t]
        running = jnp.dot(w[0], lo_t, preferred_element_type=F32)
        p_out[t] = running + jnp.dot(w[1], lo_t, preferred_element_type=F32)


def piece_index(core, value, j, count):
    return jnp.where(core == 0, 2 * j + value, value * count + j)


def main_kernel(n_high, n_col, where, p_own, old, new, *refs):
    t_count = new.shape[0]
    slots = old.shape[1]
    n_far = n_high - 1
    w_ins, parts = refs[:n_far], refs[n_far:-8]
    u_keep, u_send, g_keep, g_send, lo, u_all, g_all, sems = refs[-8:]
    width = new.shape[-1]
    part_rows = slots * width
    cases = len(parts) // max(n_far, 1)
    waits = [
        fill(where, parts[g * cases : (g + 1) * cases], lo.at[g], sems.at[g]) for g in range(n_far)
    ]
    panels = []
    index = 0
    for t in range(t_count):
        running = p_own[t]
        for g in range(n_high - 1):
            waits[g](t)
            lo_t = lo[g, t]
            running += jnp.dot(w_ins[g][0], lo_t, preferred_element_type=F32)
            running += jnp.dot(w_ins[g][1], lo_t, preferred_element_type=F32)
        for s in range(t):
            running += jnp.dot(panels[s], new[t, s], preferred_element_type=F32)
        current = -running
        u_all[t] = current
        panels.append(current.astype(BF16))
        own = old[t].reshape(part_rows, width)
        for s in range(t + 1):
            left, right = (own, panels[t]) if s == t else (panels[s], own)
            g_all[pl.ds(index * width, width), :] = lax.dot_general(
                left, right, (((0,), (0,)), ((), ())), preferred_element_type=F32
            )
            index += 1
    half = g_keep.shape[0]
    g_keep[...] = g_all[pl.ds(pl.multiple_of(where[1] * half, 16), half), :]
    g_send[...] = g_all[pl.ds(pl.multiple_of((1 - where[1]) * half, 16), half), :].astype(BF16)
    share = width // n_col
    count = n_col // 2
    for value, out in ((where[4], u_keep), (1 - where[4], u_send)):
        for j in range(count):
            start = piece_index(where[1], value, j, count) * share
            for t in range(t_count):
                for s in range(slots):
                    window = pl.ds(pl.multiple_of(s * width + start, 16), share)
                    out[j, t, s] = u_all[t, window, :].astype(out.dtype)


def halving_kernel(bit, where, keep, received, keep_out, send_out):
    count = keep_out.shape[0]
    for value, out in ((where[bit], keep_out), (1 - where[bit], send_out)):
        for j in range(count):
            index = piece_index(where[1], value, j, count)
            out[j] = (keep[index] + received[index].astype(F32)).astype(out.dtype)


def split_kernel(where, keep, received, own, *sends):
    def piece(m):
        index = where[3] ^ m
        return keep[index] + received[index].astype(F32)

    own[...] = piece(0)
    for m, send in enumerate(sends):
        send[...] = piece(m + 1).astype(BF16)


def tree(values):
    while len(values) > 1:
        values = [a + b for a, b in zip(values[::2], values[1::2])]
    return values[0]


def add_kernel(*refs):
    out = refs[-1]
    out[...] = tree([ref[...].astype(F32) for ref in refs[:-1]]).astype(out.dtype)


def wide_dot(left, right, dims):
    dims = (dims, ((), ()))
    if left.dtype == F32:
        high = left.astype(BF16)
        low = (left - high.astype(F32)).astype(BF16)
        return lax.dot_general(high, right, dims, preferred_element_type=F32) + lax.dot_general(
            low, right, dims, preferred_element_type=F32
        )
    high = right.astype(BF16)
    low = (right - high.astype(F32)).astype(BF16)
    return lax.dot_general(left, high, dims, preferred_element_type=F32) + lax.dot_general(
        left, low, dims, preferred_element_type=F32
    )


def final_kernel(where, new, diag, *refs):
    pieces, (out, g_all, y, zero, sems) = refs[:-5], refs[-5:]
    t_count = new.shape[0]
    width = new.shape[-1]
    n_plane = len(pieces) // 2
    rows = pieces[0].shape[0]
    for i, piece in enumerate(pieces):
        core, chip = where[1] ^ i // n_plane, where[3] ^ i % n_plane
        place = (core * n_plane + chip) * rows
        g_all[pl.ds(pl.multiple_of(place, 16), rows), :] = piece[...]

    def g(t, s):
        index = t * (t + 1) // 2 + s
        return g_all[pl.ds(index * width, width), :].astype(F32)

    def give(source, t, s):
        copy = pltpu.make_async_copy(source, out.at[t, s], sems.at[t, s])
        copy.start()
        sent.append(copy)

    sent = []
    zero[...] = jnp.zeros_like(zero)
    for t in range(t_count):
        for s in range(t + 1, t_count):
            give(zero, t, s)
    blocks = {}
    for t in range(t_count):
        for s in range(t):
            crossed = g(t, s)
            for u in range(t):
                if u >= s:
                    crossed += wide_dot(blocks[u, s], new[t, u], ((1,), (0,)))
                else:
                    crossed += wide_dot(blocks[s, u], new[t, u], ((0,), (0,)))
            blocks[t, s] = -crossed
            y[t, s] = blocks[t, s]
            give(y.at[t, s], t, s)
        diagonal = diag[t] - g(t, t)
        for s in range(t):
            diagonal -= wide_dot(new[t, s], blocks[t, s], ((0,), (0,)))
        blocks[t, t] = diagonal
        y[t, t] = diagonal
        give(y.at[t, t], t, t)
    for copy in sent:
        copy.wait()


def call(kernel, shapes, in_specs, scratch=(), flops=0, moved=0, limit=8):
    def place(shape):
        if not isinstance(shape, jax.ShapeDtypeStruct):
            return ANY
        return SMEM if shape.dtype == jnp.int32 else VMEM

    return pl.pallas_call(
        kernel,
        out_shape=shapes,
        in_specs=in_specs,
        out_specs=tuple(map(place, shapes)) if isinstance(shapes, tuple) else place(shapes),
        scratch_shapes=list(scratch),
        cost_estimate=pl.CostEstimate(flops=flops, bytes_accessed=moved, transcendentals=0),
        compiler_params=pltpu.CompilerParams(vmem_limit_bytes=limit << 20),
    )


def per_device(
    inverse_blocks,
    inverse_rows,
    inverse_cols,
    inverse_count,
    panel_rows,
    lower_old,
    lower_new,
    diag_inverse,
):
    blocks = inverse_blocks[0]
    kmax = blocks.shape[0]
    width = blocks.shape[-1]
    t_count, slots = lower_old.shape[:2]
    n_row = lax.axis_size("row")
    n_col = lax.axis_size("col")
    row_me = lax.axis_index("row")
    col_me = lax.axis_index("col")
    devices = [(r, c) for r in range(n_row) for c in range(n_col)]
    n_high = n_row // n_col
    n_plane = n_row // 2

    def pairs(active, partner):
        return [
            (r * n_col + c, pr * n_col + pc)
            for r, c in devices
            if active(r, c)
            for pr, pc in [partner(r, c)]
        ]

    high_me = row_me // n_col
    groups = [((high_me ^ g) * n_col + col_me) for g in range(n_high)]
    n_cand = n_high * slots
    me = jnp.stack([row_me, *groups]).astype(jnp.int32)
    source = (row_me ^ col_me) & (n_col - 1)
    core_me = row_me & 1
    chip_me = row_me >> 1
    col_bits = n_col.bit_length() - 1

    def bit_of(value, bits, i):
        return jnp.where(core_me == 0, value >> i, value >> bits - 1 - i) & 1

    where = jnp.stack(
        [source, core_me, col_me, chip_me] + [bit_of(col_me, col_bits, i) for i in range(col_bits)]
    ).astype(jnp.int32)

    block = width * width
    anyone = lambda r, c: True

    def core_swap(value):
        return permute(value, pairs(anyone, lambda r, c: (r ^ 1, c)))

    def spread(group, offset, core, land=0):
        table = {}
        for r, c in devices:
            if r % n_col == c:
                table[r ^ core, c] = ((r // n_col ^ group) * n_col + (c ^ offset) ^ land, c)
        targets = set(table.values())
        for r, c in devices:
            if (r ^ c) & 1 == 0:
                for taker in (r, r ^ 1):
                    for giver in (taker ^ 1, taker) if core else (taker ^ 1,):
                        if (giver, c) not in table and (taker, c) not in targets:
                            table[giver, c] = (taker, c)
                            targets.add((taker, c))
        return [(r * n_col + c, pr * n_col + pc) for (r, c), (pr, pc) in table.items()]

    offsets = list(range(0, n_col, 2))
    sibling = core_swap(lower_old)
    own_parts = [lower_old, sibling]
    for o in offsets[1:]:
        part = permute(lower_old, spread(0, o, 0))
        own_parts += [part, core_swap(part)]
    far = {}
    for g in range(1, n_high):
        far[g, 0] = permute(lower_old, spread(g, 0, 0, 1))
    for g in range(1, n_high):
        for o in offsets[1:]:
            far[g, o] = permute(sibling, spread(g, o, 1))
    far_parts = []
    for g in range(1, n_high):
        for o in offsets:
            both = [far[g, o], core_swap(far[g, o])]
            far_parts += both if o else both[::-1]

    w_shape = (2, slots * width, slots * width)
    ws = call(
        functools.partial(gather_kernel, n_high, slots),
        (pltpu.MemorySpace.HBM(w_shape, BF16),) * n_high,
        [SMEM, SMEM] + [ANY] * 4,
        [
            pltpu.VMEM((slots * n_cand, width, width), F32),
            pltpu.VMEM((n_high, *w_shape), BF16),
            pltpu.SMEM((kmax,), jnp.int32),
            pltpu.SMEM((kmax,), jnp.int32),
            pltpu.VMEM((DEPTH, width, width), BF16),
            pltpu.SMEM(inverse_rows.shape, jnp.int32),
            pltpu.SMEM(inverse_cols.shape, jnp.int32),
            pltpu.SMEM(panel_rows.shape, jnp.int32),
            pltpu.SemaphoreType.DMA((DEPTH,)),
            pltpu.SemaphoreType.DMA((n_high,)),
            pltpu.SemaphoreType.DMA((3,)),
        ],
        flops=block * 16,
        moved=16 * block * 2 + 16 * n_cand * slots * block,
        limit=6 + (slots * n_cand * 8 * block + DEPTH * 2 * block) // 2**20,
    )(
        me,
        inverse_count,
        *[
            pltpu.with_memory_space_constraint(value, pltpu.MemorySpace.HBM)
            for value in (inverse_rows, inverse_cols, panel_rows, blocks)
        ],
    )
    p_shape = (t_count, slots * width, width)
    p_own = call(
        own_kernel,
        jax.ShapeDtypeStruct(p_shape, F32),
        [SMEM, ANY] + [ANY] * len(own_parts),
        [
            pltpu.VMEM(w_shape, BF16),
            pltpu.VMEM(p_shape, BF16),
            pltpu.SemaphoreType.DMA,
            pltpu.SemaphoreType.DMA((t_count, slots)),
        ],
        flops=4 * block * width * slots * slots * t_count,
        moved=8 * block * t_count * slots,
        limit=12,
    )(
        where,
        pltpu.with_memory_space_constraint(ws[0], pltpu.MemorySpace.HBM),
        *own_parts,
    )

    share = width // n_col
    n_blocks = t_count * (t_count + 1) // 2
    half = n_blocks * width // 2
    piece = half // n_plane
    u_shape = (n_col // 2, t_count, slots, share, width)
    u_keep, u_send, g_keep, g_send = call(
        functools.partial(main_kernel, n_high, n_col),
        (
            jax.ShapeDtypeStruct(u_shape, F32),
            jax.ShapeDtypeStruct(u_shape, BF16),
            jax.ShapeDtypeStruct((half, width), F32),
            jax.ShapeDtypeStruct((half, width), BF16),
        ),
        [SMEM, VMEM, VMEM, VMEM] + [VMEM] * (n_high - 1) + [ANY] * len(far_parts),
        [
            pltpu.VMEM((n_high - 1, t_count, slots * width, width), BF16),
            pltpu.VMEM((t_count, slots * width, width), F32),
            pltpu.VMEM((n_blocks * width, width), F32),
            pltpu.SemaphoreType.DMA((n_high - 1, t_count, slots)),
        ],
        flops=2 * block * width * slots * t_count * (2 * n_cand + 4),
        moved=4 * block * t_count * n_cand,
        limit=12 + 2 * n_high,
    )(where, p_own, lower_old, lower_new, *ws[1:], *far_parts)

    def step(index):
        return pairs(
            anyone, lambda r, c: (r, c ^ 1 << (index if r & 1 == 0 else col_bits - 1 - index))
        )

    def halve(position, keep, received):
        shape = (keep.shape[0] // 2, *keep.shape[1:])
        return call(
            functools.partial(halving_kernel, position),
            (jax.ShapeDtypeStruct(shape, F32), jax.ShapeDtypeStruct(shape, BF16)),
            [SMEM, VMEM, VMEM],
            flops=keep.size,
            moved=keep.size * 6,
        )(where, keep, received)

    def add(dtype, values):
        return call(
            add_kernel,
            jax.ShapeDtypeStruct(values[0].shape, dtype),
            [VMEM] * len(values),
            flops=len(values) * values[0].size,
            moved=values[0].size * 2 * len(values),
        )(*values)

    keep = g_keep.reshape(n_plane, piece, width)
    received = core_swap(g_send)
    u_received = permute(u_send, step(0))
    shape = (piece, width)
    own, *sends = call(
        split_kernel,
        (jax.ShapeDtypeStruct(shape, F32), *[jax.ShapeDtypeStruct(shape, BF16)] * (n_plane - 1)),
        [SMEM, VMEM, VMEM],
        flops=half * width,
        moved=half * width * 8,
    )(where, keep, received.reshape(keep.shape))
    arrived = [
        permute(send, pairs(anyone, lambda r, c: (r ^ 2 * (m + 1), c)))
        for m, send in enumerate(sends)
    ]
    in_plane = add(BF16, [own, *arrived])
    level = [in_plane] + [
        permute(in_plane, pairs(anyone, lambda r, c: (r, c ^ m))) for m in range(1, n_col)
    ]
    for i in range(1, col_bits):
        u_keep, u_send = halve(5 + i - 1, u_keep, u_received)
        u_received = permute(u_send, step(i))
    total = add(BF16, level)
    pieces = [total] + [
        permute(total, pairs(anyone, lambda r, c: (r ^ 2 * m, c))) for m in range(1, n_plane)
    ]
    pieces += [core_swap(value) for value in pieces]
    supernode_inverse = call(
        final_kernel,
        pltpu.MemorySpace.HBM((t_count, t_count, width, width), F32),
        [SMEM] + [VMEM] * (2 + len(pieces)),
        [
            pltpu.VMEM((n_blocks * width, width), BF16),
            pltpu.VMEM((t_count, t_count, width, width), F32),
            pltpu.VMEM((width, width), F32),
            pltpu.SemaphoreType.DMA((t_count, t_count)),
        ],
        flops=2 * block * width * 16,
        moved=block * t_count * t_count * 6,
    )(where, lower_new, diag_inverse, *pieces)
    panel_inverse = add(BF16, [u_keep, u_received])[0]
    return (panel_inverse, supernode_inverse)


def solution(mesh):
    placed = (
        P("row", "col", None, None),
        P("row", "col"),
        P("row", "col"),
        P("row", "col"),
        P(),
        P(None, "row", None, None),
        P(),
        P(),
    )
    return jax.shard_map(
        per_device,
        mesh=mesh,
        in_specs=placed,
        out_specs=(P(None, "row", "col", None), P()),
        check_vma=False,
    )
```

```python
import functools

import jax
import jax.numpy as jnp
from jax import lax
from jax.experimental import pallas as pl
from jax.experimental.pallas import tpu as pltpu
from jax.sharding import PartitionSpec as P


BF16 = jnp.bfloat16
F32 = jnp.float32
VMEM = pl.BlockSpec(memory_space=pltpu.VMEM)
ANY = pl.BlockSpec(memory_space=pl.ANY)
SMEM = pl.BlockSpec(memory_space=pltpu.SMEM)
DEPTH = 8


def permute(value, pairs):
    return lax.ppermute(value, ("row", "col"), pairs)


def gather_kernel(groups, slots, me, count, rows_in, cols_in, panel_in, blocks, *refs):
    w_outs = refs[:groups]
    acc, w, order, code, buf, rows_ref, cols_ref, panel, sem, out_sem, in_sem = refs[groups:]
    width = buf.shape[-1]
    n_cand = groups * slots
    row_me = me[0]
    tables = ((rows_in, rows_ref), (cols_in, cols_ref), (panel_in, panel))
    brought = [pltpu.make_async_copy(*pair, in_sem.at[i]) for i, pair in enumerate(tables)]
    for copy in brought:
        copy.start()
    acc[...] = jnp.zeros_like(acc)
    for copy in brought:
        copy.wait()
    own = [panel[row_me * slots + s] for s in range(slots)]
    cand = [panel[me[1 + g] * slots + s] for g in range(groups) for s in range(slots)]
    step_size = 8 if rows_ref.shape[1] % 8 == 0 else 1

    def scan(step, n):
        for u in range(step_size):
            k = step * step_size + u
            row, col = rows_ref[0, k], cols_ref[0, k]
            where = jnp.int32(-1)
            for p in range(n_cand):
                where = jnp.where(col == cand[p], p, where)
            slot = jnp.int32(-1)
            for s in range(slots):
                slot = jnp.where(row == own[s], s, slot)
            order[n] = k
            code[n] = slot * n_cand + where
            used = (where >= 0) & (slot >= 0) & (k < count[0, 0])
            n = n + used.astype(jnp.int32)
        return n

    n_steps = (count[0, 0] + step_size - 1) // step_size
    n_used = lax.fori_loop(0, n_steps, scan, jnp.int32(0))

    def fetch(i):
        slot = lax.rem(i, DEPTH)
        return pltpu.make_async_copy(blocks.at[order[i]], buf.at[slot], sem.at[slot])

    for i in range(DEPTH):

        @pl.when(i < n_used)
        def _():
            fetch(jnp.int32(i)).start()

    def step(i, carry):
        fetch(i).wait()
        target = code[i]
        slot = lax.rem(i, DEPTH)
        acc[target] += buf[slot].astype(F32)

        @pl.when(i + DEPTH < n_used)
        def _():
            fetch(i + DEPTH).start()

        return carry

    lax.fori_loop(0, n_used, step, 0)
    for g in range(groups):
        for s in range(slots):
            for p in range(slots):
                rows = pl.ds(s * width, width)
                cols = pl.ds(p * width, width)
                value = acc[s * n_cand + g * slots + p]
                high = value.astype(BF16)
                w[g, 0, rows, cols] = high
                w[g, 1, rows, cols] = (value - high.astype(F32)).astype(BF16)
        pltpu.make_async_copy(w.at[g], w_outs[g], out_sem.at[g]).start()
    for g in range(groups):
        pltpu.make_async_copy(w.at[g], w_outs[g], out_sem.at[g]).wait()


def fill(where, options, lo, sems):
    count, slots, width = options[0].shape[:3]

    def copies(part, t):
        return [
            pltpu.make_async_copy(
                part.at[t, p], lo.at[t, pl.ds(p * width, width), :], sems.at[t, p]
            )
            for p in range(slots)
        ]

    for case, part in enumerate(options):

        @pl.when(where[0] == case)
        def _():
            for t in range(count):
                for copy in copies(part, t):
                    copy.start()

    def wait(t):
        for copy in copies(options[0], t):
            copy.wait()

    return wait


def stacked_dot(w, panel):
    both = jnp.dot(w.reshape(-1, w.shape[-1]), panel, preferred_element_type=F32)
    return both[: w.shape[1]] + both[w.shape[1] :]


def own_kernel(where, w_in, old, *refs):
    options, (p_out, old_out, w, lo, w_sem, sems) = refs[:-6], refs[-6:]
    w_copy = pltpu.make_async_copy(w_in, w, w_sem)
    w_copy.start()
    wait = fill(where, options, lo, sems)
    for t in range(lo.shape[0]):
        old_out[t] = old[t].reshape(lo.shape[1:]).T
    w_copy.wait()
    for t in range(lo.shape[0]):
        wait(t)
        p_out[t] = stacked_dot(w[...], lo[t])


def piece_index(core, value, j, count):
    return jnp.where(core == 0, 2 * j + value, value * count + j)


def main_kernel(n_high, n_col, where, p_own, old_t, new, *refs):
    t_count = new.shape[0]
    width = new.shape[-1]
    slots = old_t.shape[-1] // width
    n_far = n_high - 1
    w_ins, parts = refs[:n_far], refs[n_far:-8]
    u_keep, u_send, g_keep, g_send, lo, u_all, g_all, sems = refs[-8:]
    cases = len(parts) // max(n_far, 1)
    waits = [
        fill(where, parts[g * cases : (g + 1) * cases], lo.at[g], sems.at[g]) for g in range(n_far)
    ]
    for t in range(t_count):
        for wait in waits:
            wait(t)
    totals = [
        p_own[t] + sum(stacked_dot(w_ins[g][...], lo[g, t]) for g in range(n_far))
        for t in range(t_count)
    ]
    for s in range(t_count):
        u_all[s] = -totals[s]
        panel = (-totals[s]).astype(BF16)
        for t in range(s + 1, t_count):
            totals[t] += jnp.dot(panel, new[t, s], preferred_element_type=F32)
        rest = old_t[s:].reshape(-1, old_t.shape[-1])
        crossed = jnp.dot(rest, panel, preferred_element_type=F32)
        for t in range(s, t_count):
            g_all[pl.ds((t * (t + 1) // 2 + s) * width, width), :] = crossed[
                (t - s) * width : (t - s + 1) * width
            ]
    half = g_keep.shape[0]
    g_keep[...] = g_all[pl.ds(pl.multiple_of(where[1] * half, 16), half), :]
    g_send[...] = g_all[pl.ds(pl.multiple_of((1 - where[1]) * half, 16), half), :].astype(BF16)
    share = width // n_col
    count = n_col // 2
    for value, out in ((where[4], u_keep), (1 - where[4], u_send)):
        for j in range(count):
            start = piece_index(where[1], value, j, count) * share
            for t in range(t_count):
                for s in range(slots):
                    window = pl.ds(pl.multiple_of(s * width + start, 16), share)
                    out[j, t, s] = u_all[t, window, :].astype(out.dtype)


def halving_kernel(bit, where, keep, received, keep_out, send_out):
    count = keep_out.shape[0]
    for value, out in ((where[bit], keep_out), (1 - where[bit], send_out)):
        for j in range(count):
            index = piece_index(where[1], value, j, count)
            out[j] = (keep[index] + received[index].astype(F32)).astype(out.dtype)


def split_kernel(where, keep, received, own, *sends):
    def piece(m):
        index = where[3] ^ m
        return keep[index] + received[index].astype(F32)

    own[...] = piece(0)
    for m, send in enumerate(sends):
        send[...] = piece(m + 1).astype(BF16)


def tree(values):
    while len(values) > 1:
        values = [a + b for a, b in zip(values[::2], values[1::2])]
    return values[0]


def add_kernel(*refs):
    out = refs[-1]
    out[...] = tree([ref[...].astype(F32) for ref in refs[:-1]]).astype(out.dtype)


def wide_dot(left, right, dims):
    wide = left if left.dtype == F32 else right
    high = wide.astype(BF16)
    low = (wide - high.astype(F32)).astype(BF16)
    if left.dtype == F32:
        axis = 1 - dims[0][0]
        both = lax.dot_general(
            jnp.concatenate([high, low], axis),
            right,
            (dims, ((), ())),
            preferred_element_type=F32,
        )
        return both[: left.shape[axis]] + both[left.shape[axis] :]
    parts = [
        lax.dot_general(left, part, (dims, ((), ())), preferred_element_type=F32)
        for part in (high, low)
    ]
    return parts[0] + parts[1]


def final_kernel(where, new, diag, *refs):
    pieces, (out, g_all, y, zero, sems) = refs[:-5], refs[-5:]
    t_count = new.shape[0]
    width = new.shape[-1]
    n_plane = len(pieces) // 2
    rows = pieces[0].shape[0]
    for i, piece in enumerate(pieces):
        core, chip = where[1] ^ i // n_plane, where[3] ^ i % n_plane
        place = (core * n_plane + chip) * rows
        g_all[pl.ds(pl.multiple_of(place, 16), rows), :] = piece[...]

    def g(t, s):
        index = t * (t + 1) // 2 + s
        value = g_all[pl.ds(index * width, width), :]
        return (value if s == t else value.T).astype(F32)

    def give(source, t, s):
        copy = pltpu.make_async_copy(source, out.at[t, s], sems.at[t, s])
        copy.start()
        sent.append(copy)

    sent = []
    zero[...] = jnp.zeros_like(zero)
    for t in range(t_count):
        for s in range(t + 1, t_count):
            give(zero, t, s)
    blocks = {}
    for t in range(t_count):
        for s in range(t):
            crossed = g(t, s)
            for u in range(t):
                if u >= s:
                    crossed += wide_dot(blocks[u, s], new[t, u], ((1,), (0,)))
                else:
                    crossed += wide_dot(blocks[s, u], new[t, u], ((0,), (0,)))
            blocks[t, s] = -crossed
            y[t, s] = blocks[t, s]
            give(y.at[t, s], t, s)
        diagonal = diag[t] - g(t, t)
        for s in range(t):
            diagonal -= wide_dot(new[t, s], blocks[t, s], ((0,), (0,)))
        blocks[t, t] = diagonal
        y[t, t] = diagonal
        give(y.at[t, t], t, t)
    for copy in sent:
        copy.wait()


def call(kernel, shapes, in_specs, scratch=(), flops=0, moved=0, limit=8):
    def place(shape):
        if not isinstance(shape, jax.ShapeDtypeStruct):
            return ANY
        return SMEM if shape.dtype == jnp.int32 else VMEM

    return pl.pallas_call(
        kernel,
        out_shape=shapes,
        in_specs=in_specs,
        out_specs=tuple(map(place, shapes)) if isinstance(shapes, tuple) else place(shapes),
        scratch_shapes=list(scratch),
        cost_estimate=pl.CostEstimate(flops=flops, bytes_accessed=moved, transcendentals=0),
        compiler_params=pltpu.CompilerParams(vmem_limit_bytes=limit << 20),
    )


def per_device(
    inverse_blocks,
    inverse_rows,
    inverse_cols,
    inverse_count,
    panel_rows,
    lower_old,
    lower_new,
    diag_inverse,
):
    blocks = inverse_blocks[0]
    kmax = blocks.shape[0]
    width = blocks.shape[-1]
    t_count, slots = lower_old.shape[:2]
    n_row = lax.axis_size("row")
    n_col = lax.axis_size("col")
    row_me = lax.axis_index("row")
    col_me = lax.axis_index("col")
    devices = [(r, c) for r in range(n_row) for c in range(n_col)]
    n_high = n_row // n_col
    n_plane = n_row // 2

    def pairs(active, partner):
        return [
            (r * n_col + c, pr * n_col + pc)
            for r, c in devices
            if active(r, c)
            for pr, pc in [partner(r, c)]
        ]

    high_me = row_me // n_col
    groups = [((high_me ^ g) * n_col + col_me) for g in range(n_high)]
    n_cand = n_high * slots
    me = jnp.stack([row_me, *groups]).astype(jnp.int32)
    source = (row_me ^ col_me) & (n_col - 1)
    core_me = row_me & 1
    chip_me = row_me >> 1
    col_bits = n_col.bit_length() - 1

    def bit_of(value, bits, i):
        return jnp.where(core_me == 0, value >> i, value >> bits - 1 - i) & 1

    where = jnp.stack(
        [source, core_me, col_me, chip_me] + [bit_of(col_me, col_bits, i) for i in range(col_bits)]
    ).astype(jnp.int32)

    block = width * width
    anyone = lambda r, c: True

    def core_swap(value):
        return permute(value, pairs(anyone, lambda r, c: (r ^ 1, c)))

    def spread(group, offset, core, land=0):
        table = {}
        for r, c in devices:
            if r % n_col == c:
                table[r ^ core, c] = ((r // n_col ^ group) * n_col + (c ^ offset) ^ land, c)
        targets = set(table.values())
        for r, c in devices:
            if (r ^ c) & 1 == 0:
                for taker in (r, r ^ 1):
                    for giver in (taker ^ 1, taker) if core else (taker ^ 1,):
                        if (giver, c) not in table and (taker, c) not in targets:
                            table[giver, c] = (taker, c)
                            targets.add((taker, c))
        return [(r * n_col + c, pr * n_col + pc) for (r, c), (pr, pc) in table.items()]

    offsets = list(range(0, n_col, 2))
    sibling = core_swap(lower_old)
    own_parts = [lower_old, sibling]
    for o in offsets[1:]:
        part = permute(lower_old, spread(0, o, 0))
        own_parts += [part, core_swap(part)]
    far = {}
    for g in range(1, n_high):
        far[g, 0] = permute(lower_old, spread(g, 0, 0, 1))
    for g in range(1, n_high):
        for o in offsets[1:]:
            far[g, o] = permute(sibling, spread(g, o, 1))
    far_parts = []
    for g in range(1, n_high):
        for o in offsets:
            both = [far[g, o], core_swap(far[g, o])]
            far_parts += both if o else both[::-1]

    w_shape = (2, slots * width, slots * width)
    ws = call(
        functools.partial(gather_kernel, n_high, slots),
        (pltpu.MemorySpace.HBM(w_shape, BF16),) * n_high,
        [SMEM, SMEM] + [ANY] * 4,
        [
            pltpu.VMEM((slots * n_cand, width, width), F32),
            pltpu.VMEM((n_high, *w_shape), BF16),
            pltpu.SMEM((kmax,), jnp.int32),
            pltpu.SMEM((kmax,), jnp.int32),
            pltpu.VMEM((DEPTH, width, width), BF16),
            pltpu.SMEM(inverse_rows.shape, jnp.int32),
            pltpu.SMEM(inverse_cols.shape, jnp.int32),
            pltpu.SMEM(panel_rows.shape, jnp.int32),
            pltpu.SemaphoreType.DMA((DEPTH,)),
            pltpu.SemaphoreType.DMA((n_high,)),
            pltpu.SemaphoreType.DMA((3,)),
        ],
        flops=block * 16,
        moved=16 * block * 2 + 16 * n_cand * slots * block,
        limit=6 + (slots * n_cand * 8 * block + DEPTH * 2 * block) // 2**20,
    )(
        me,
        inverse_count,
        *[
            pltpu.with_memory_space_constraint(value, pltpu.MemorySpace.HBM)
            for value in (inverse_rows, inverse_cols, panel_rows, blocks)
        ],
    )
    p_shape = (t_count, slots * width, width)
    p_own, old_t = call(
        own_kernel,
        (
            jax.ShapeDtypeStruct(p_shape, F32),
            jax.ShapeDtypeStruct((t_count, width, slots * width), BF16),
        ),
        [SMEM, ANY, VMEM] + [ANY] * len(own_parts),
        [
            pltpu.VMEM(w_shape, BF16),
            pltpu.VMEM(p_shape, BF16),
            pltpu.SemaphoreType.DMA,
            pltpu.SemaphoreType.DMA((t_count, slots)),
        ],
        flops=4 * block * width * slots * slots * t_count,
        moved=8 * block * t_count * slots,
        limit=12,
    )(
        where,
        pltpu.with_memory_space_constraint(ws[0], pltpu.MemorySpace.HBM),
        lower_old,
        *own_parts,
    )

    share = width // n_col
    n_blocks = t_count * (t_count + 1) // 2
    half = n_blocks * width // 2
    piece = half // n_plane
    u_shape = (n_col // 2, t_count, slots, share, width)
    u_keep, u_send, g_keep, g_send = call(
        functools.partial(main_kernel, n_high, n_col),
        (
            jax.ShapeDtypeStruct(u_shape, F32),
            jax.ShapeDtypeStruct(u_shape, BF16),
            jax.ShapeDtypeStruct((half, width), F32),
            jax.ShapeDtypeStruct((half, width), BF16),
        ),
        [SMEM, VMEM, VMEM, VMEM] + [VMEM] * (n_high - 1) + [ANY] * len(far_parts),
        [
            pltpu.VMEM((n_high - 1, t_count, slots * width, width), BF16),
            pltpu.VMEM((t_count, slots * width, width), F32),
            pltpu.VMEM((n_blocks * width, width), F32),
            pltpu.SemaphoreType.DMA((n_high - 1, t_count, slots)),
        ],
        flops=2 * block * width * slots * t_count * (2 * n_cand + 4),
        moved=4 * block * t_count * n_cand,
        limit=12 + 2 * n_high,
    )(where, p_own, old_t, lower_new, *ws[1:], *far_parts)

    def step(index):
        return pairs(
            anyone, lambda r, c: (r, c ^ 1 << (index if r & 1 == 0 else col_bits - 1 - index))
        )

    def halve(position, keep, received):
        shape = (keep.shape[0] // 2, *keep.shape[1:])
        return call(
            functools.partial(halving_kernel, position),
            (jax.ShapeDtypeStruct(shape, F32), jax.ShapeDtypeStruct(shape, BF16)),
            [SMEM, VMEM, VMEM],
            flops=keep.size,
            moved=keep.size * 6,
        )(where, keep, received)

    def add(dtype, values):
        return call(
            add_kernel,
            jax.ShapeDtypeStruct(values[0].shape, dtype),
            [VMEM] * len(values),
            flops=len(values) * values[0].size,
            moved=values[0].size * 2 * len(values),
        )(*values)

    keep = g_keep.reshape(n_plane, piece, width)
    received = core_swap(g_send)
    u_received = permute(u_send, step(0))
    shape = (piece, width)
    own, *sends = call(
        split_kernel,
        (jax.ShapeDtypeStruct(shape, F32), *[jax.ShapeDtypeStruct(shape, BF16)] * (n_plane - 1)),
        [SMEM, VMEM, VMEM],
        flops=half * width,
        moved=half * width * 8,
    )(where, keep, received.reshape(keep.shape))
    arrived = [
        permute(send, pairs(anyone, lambda r, c: (r ^ 2 * (m + 1), c)))
        for m, send in enumerate(sends)
    ]
    in_plane = add(BF16, [own, *arrived])
    level = [in_plane] + [
        permute(in_plane, pairs(anyone, lambda r, c: (r, c ^ m))) for m in range(1, n_col)
    ]
    for i in range(1, col_bits):
        u_keep, u_send = halve(5 + i - 1, u_keep, u_received)
        u_received = permute(u_send, step(i))
    total = add(BF16, level)
    pieces = [total] + [
        permute(total, pairs(anyone, lambda r, c: (r ^ 2 * m, c))) for m in range(1, n_plane)
    ]
    pieces += [core_swap(value) for value in pieces]
    supernode_inverse = call(
        final_kernel,
        pltpu.MemorySpace.HBM((t_count, t_count, width, width), F32),
        [SMEM] + [VMEM] * (2 + len(pieces)),
        [
            pltpu.VMEM((n_blocks * width, width), BF16),
            pltpu.VMEM((t_count, t_count, width, width), F32),
            pltpu.VMEM((width, width), F32),
            pltpu.SemaphoreType.DMA((t_count, t_count)),
        ],
        flops=2 * block * width * 16,
        moved=block * t_count * t_count * 6,
    )(where, lower_new, diag_inverse, *pieces)
    panel_inverse = add(BF16, [u_keep, u_received])[0]
    return (panel_inverse, supernode_inverse)


def solution(mesh):
    placed = (
        P("row", "col", None, None),
        P("row", "col"),
        P("row", "col"),
        P("row", "col"),
        P(),
        P(None, "row", None, None),
        P(),
        P(),
    )
    return jax.shard_map(
        per_device,
        mesh=mesh,
        in_specs=placed,
        out_specs=(P(None, "row", "col", None), P()),
        check_vma=False,
    )
```

```python
import functools

import jax
import jax.numpy as jnp
from jax import lax
from jax.experimental import pallas as pl
from jax.experimental.pallas import tpu as pltpu
from jax.sharding import PartitionSpec as P


BF16 = jnp.bfloat16
F32 = jnp.float32
VMEM = pl.BlockSpec(memory_space=pltpu.VMEM)
ANY = pl.BlockSpec(memory_space=pl.ANY)
SMEM = pl.BlockSpec(memory_space=pltpu.SMEM)
DEPTH = 8


def permute(value, pairs):
    return lax.ppermute(value, ("row", "col"), pairs)


def gather_kernel(groups, slots, me, count, rows_in, cols_in, panel_in, blocks, *refs):
    w_outs = refs[:groups]
    acc, w, order, code, buf, rows_ref, cols_ref, panel, sem, out_sem, in_sem = refs[groups:]
    width = buf.shape[-1]
    n_cand = groups * slots
    row_me = me[0]
    tables = ((rows_in, rows_ref), (cols_in, cols_ref), (panel_in, panel))
    brought = [pltpu.make_async_copy(*pair, in_sem.at[i]) for i, pair in enumerate(tables)]
    for copy in brought:
        copy.start()
    acc[...] = jnp.zeros_like(acc)
    for copy in brought:
        copy.wait()
    own = [panel[row_me * slots + s] for s in range(slots)]
    cand = [panel[me[1 + g] * slots + s] for g in range(groups) for s in range(slots)]
    step_size = 8 if rows_ref.shape[1] % 8 == 0 else 1

    def scan(step, n):
        for u in range(step_size):
            k = step * step_size + u
            row, col = rows_ref[0, k], cols_ref[0, k]
            where = jnp.int32(-1)
            for p in range(n_cand):
                where = jnp.where(col == cand[p], p, where)
            slot = jnp.int32(-1)
            for s in range(slots):
                slot = jnp.where(row == own[s], s, slot)
            order[n] = k
            code[n] = slot * n_cand + where
            used = (where >= 0) & (slot >= 0) & (k < count[0, 0])
            n = n + used.astype(jnp.int32)
        return n

    n_steps = (count[0, 0] + step_size - 1) // step_size
    n_used = lax.fori_loop(0, n_steps, scan, jnp.int32(0))

    def fetch(i):
        slot = lax.rem(i, DEPTH)
        return pltpu.make_async_copy(blocks.at[order[i]], buf.at[slot], sem.at[slot])

    for i in range(DEPTH):

        @pl.when(i < n_used)
        def _():
            fetch(jnp.int32(i)).start()

    def step(i, carry):
        fetch(i).wait()
        target = code[i]
        slot = lax.rem(i, DEPTH)
        acc[target] += buf[slot].astype(F32)

        @pl.when(i + DEPTH < n_used)
        def _():
            fetch(i + DEPTH).start()

        return carry

    lax.fori_loop(0, n_used, step, 0)
    for g in range(groups):
        for s in range(slots):
            for p in range(slots):
                rows = pl.ds(s * width, width)
                cols = pl.ds(p * width, width)
                value = acc[s * n_cand + g * slots + p]
                high = value.astype(BF16)
                w[g, 0, rows, cols] = high
                w[g, 1, rows, cols] = (value - high.astype(F32)).astype(BF16)
        pltpu.make_async_copy(w.at[g], w_outs[g], out_sem.at[g]).start()
    for g in range(groups):
        pltpu.make_async_copy(w.at[g], w_outs[g], out_sem.at[g]).wait()


def fill(where, options, lo, sems):
    count, slots, width = options[0].shape[:3]

    def copies(part, t):
        return [
            pltpu.make_async_copy(
                part.at[t, p], lo.at[t, pl.ds(p * width, width), :], sems.at[t, p]
            )
            for p in range(slots)
        ]

    for case, part in enumerate(options):

        @pl.when(where[0] == case)
        def _():
            for t in range(count):
                for copy in copies(part, t):
                    copy.start()

    def wait(t):
        for copy in copies(options[0], t):
            copy.wait()

    return wait


def stacked_dot(w, panel):
    both = jnp.dot(w.reshape(-1, w.shape[-1]), panel, preferred_element_type=F32)
    return both[: w.shape[1]] + both[w.shape[1] :]


def own_kernel(where, w_in, old, *refs):
    options, (p_out, old_out, w, lo, w_sem, sems) = refs[:-6], refs[-6:]
    w_copy = pltpu.make_async_copy(w_in, w, w_sem)
    w_copy.start()
    wait = fill(where, options, lo, sems)
    for t in range(lo.shape[0]):
        old_out[t] = old[t].reshape(lo.shape[1:]).T
    w_copy.wait()
    for t in range(lo.shape[0]):
        wait(t)
        p_out[t] = stacked_dot(w[...], lo[t])


def piece_index(core, value, j, count):
    return jnp.where(core == 0, 2 * j + value, value * count + j)


def main_kernel(n_high, n_col, where, p_own, old_t, new, *refs):
    t_count = new.shape[0]
    width = new.shape[-1]
    slots = old_t.shape[-1] // width
    n_far = n_high - 1
    w_ins, parts = refs[:n_far], refs[n_far:-8]
    u_keep, u_send, g_keep, g_send, lo, u_all, g_all, sems = refs[-8:]
    cases = len(parts) // max(n_far, 1)
    waits = [
        fill(where, parts[g * cases : (g + 1) * cases], lo.at[g], sems.at[g]) for g in range(n_far)
    ]
    for t in range(t_count):
        for wait in waits:
            wait(t)
    totals = [
        p_own[t] + sum(stacked_dot(w_ins[g][...], lo[g, t]) for g in range(n_far))
        for t in range(t_count)
    ]
    for s in range(t_count):
        u_all[s] = -totals[s]
        panel = (-totals[s]).astype(BF16)
        for t in range(s + 1, t_count):
            totals[t] += jnp.dot(panel, new[t, s], preferred_element_type=F32)
        rest = old_t[s:].reshape(-1, old_t.shape[-1])
        crossed = jnp.dot(rest, panel, preferred_element_type=F32)
        for t in range(s, t_count):
            g_all[pl.ds((t * (t + 1) // 2 + s) * width, width), :] = crossed[
                (t - s) * width : (t - s + 1) * width
            ]
    half = g_keep.shape[0]
    g_keep[...] = g_all[pl.ds(pl.multiple_of(where[1] * half, 16), half), :]
    g_send[...] = g_all[pl.ds(pl.multiple_of((1 - where[1]) * half, 16), half), :].astype(BF16)
    share = width // n_col
    count = n_col // 2
    for value, out in ((where[4], u_keep), (1 - where[4], u_send)):
        for j in range(count):
            start = piece_index(where[1], value, j, count) * share
            for t in range(t_count):
                for s in range(slots):
                    window = pl.ds(pl.multiple_of(s * width + start, 16), share)
                    out[j, t, s] = u_all[t, window, :].astype(out.dtype)


def halving_kernel(bit, where, keep, received, keep_out, send_out):
    count = keep_out.shape[0]
    for value, out in ((where[bit], keep_out), (1 - where[bit], send_out)):
        for j in range(count):
            index = piece_index(where[1], value, j, count)
            out[j] = (keep[index] + received[index].astype(F32)).astype(out.dtype)


def split_kernel(where, keep, received, own, *sends):
    def piece(m):
        index = where[3] ^ m
        return keep[index] + received[index].astype(F32)

    own[...] = piece(0)
    for m, send in enumerate(sends):
        send[...] = piece(m + 1).astype(BF16)


def tree(values):
    while len(values) > 1:
        values = [a + b for a, b in zip(values[::2], values[1::2])]
    return values[0]


def add_kernel(*refs):
    out = refs[-1]
    out[...] = tree([ref[...].astype(F32) for ref in refs[:-1]]).astype(out.dtype)


def wide_dot(left, right, dims):
    wide = left if left.dtype == F32 else right
    high = wide.astype(BF16)
    low = (wide - high.astype(F32)).astype(BF16)
    if left.dtype == F32:
        axis = 1 - dims[0][0]
        both = lax.dot_general(
            jnp.concatenate([high, low], axis),
            right,
            (dims, ((), ())),
            preferred_element_type=F32,
        )
        return both[: left.shape[axis]] + both[left.shape[axis] :]
    parts = [
        lax.dot_general(left, part, (dims, ((), ())), preferred_element_type=F32)
        for part in (high, low)
    ]
    return parts[0] + parts[1]


def final_kernel(where, new, diag, *refs):
    pieces, (out, g_all, y, zero, sems) = refs[:-5], refs[-5:]
    t_count = new.shape[0]
    width = new.shape[-1]
    n_plane = len(pieces) // 2
    rows = pieces[0].shape[0]
    for i, piece in enumerate(pieces):
        core, chip = where[1] ^ i // n_plane, where[3] ^ i % n_plane
        place = (core * n_plane + chip) * rows
        g_all[pl.ds(pl.multiple_of(place, 16), rows), :] = piece[...]

    def g(t, s):
        index = t * (t + 1) // 2 + s
        value = g_all[pl.ds(index * width, width), :]
        return (value if s == t else value.T).astype(F32)

    def give(source, t, s):
        copy = pltpu.make_async_copy(source, out.at[t, s], sems.at[t, s])
        copy.start()
        sent.append(copy)

    sent = []
    zero[...] = jnp.zeros_like(zero)
    for t in range(t_count):
        for s in range(t + 1, t_count):
            give(zero, t, s)
    blocks = {}
    for t in range(t_count):
        for s in range(t):
            crossed = g(t, s)
            for u in range(t):
                if u >= s:
                    crossed += wide_dot(blocks[u, s], new[t, u], ((1,), (0,)))
                else:
                    crossed += wide_dot(blocks[s, u], new[t, u], ((0,), (0,)))
            blocks[t, s] = -crossed
            y[t, s] = blocks[t, s]
            give(y.at[t, s], t, s)
        diagonal = diag[t] - g(t, t)
        for s in range(t):
            diagonal -= wide_dot(new[t, s], blocks[t, s], ((0,), (0,)))
        blocks[t, t] = diagonal
        y[t, t] = diagonal
        give(y.at[t, t], t, t)
    for copy in sent:
        copy.wait()


def call(kernel, shapes, in_specs, scratch=(), flops=0, moved=0, limit=8):
    def place(shape):
        if not isinstance(shape, jax.ShapeDtypeStruct):
            return ANY
        return SMEM if shape.dtype == jnp.int32 else VMEM

    return pl.pallas_call(
        kernel,
        out_shape=shapes,
        in_specs=in_specs,
        out_specs=tuple(map(place, shapes)) if isinstance(shapes, tuple) else place(shapes),
        scratch_shapes=list(scratch),
        cost_estimate=pl.CostEstimate(flops=flops, bytes_accessed=moved, transcendentals=0),
        compiler_params=pltpu.CompilerParams(vmem_limit_bytes=limit << 20),
    )


def per_device(
    inverse_blocks,
    inverse_rows,
    inverse_cols,
    inverse_count,
    panel_rows,
    lower_old,
    lower_new,
    diag_inverse,
):
    blocks = inverse_blocks[0]
    kmax = blocks.shape[0]
    width = blocks.shape[-1]
    t_count, slots = lower_old.shape[:2]
    n_row = lax.axis_size("row")
    n_col = lax.axis_size("col")
    row_me = lax.axis_index("row")
    col_me = lax.axis_index("col")
    devices = [(r, c) for r in range(n_row) for c in range(n_col)]
    n_high = n_row // n_col
    n_plane = n_row // 2

    def pairs(active, partner):
        return [
            (r * n_col + c, pr * n_col + pc)
            for r, c in devices
            if active(r, c)
            for pr, pc in [partner(r, c)]
        ]

    high_me = row_me // n_col
    groups = [((high_me ^ g) * n_col + col_me) for g in range(n_high)]
    n_cand = n_high * slots
    me = jnp.stack([row_me, *groups]).astype(jnp.int32)
    source = (row_me ^ col_me) & (n_col - 1)
    core_me = row_me & 1
    chip_me = row_me >> 1
    col_bits = n_col.bit_length() - 1

    def bit_of(value, bits, i):
        return jnp.where(core_me == 0, value >> i, value >> bits - 1 - i) & 1

    where = jnp.stack(
        [source, core_me, col_me, chip_me] + [bit_of(col_me, col_bits, i) for i in range(col_bits)]
    ).astype(jnp.int32)

    block = width * width
    anyone = lambda r, c: True

    def core_swap(value):
        return permute(value, pairs(anyone, lambda r, c: (r ^ 1, c)))

    def spread(group, offset, core, land=0):
        table = {}
        for r, c in devices:
            if r % n_col == c:
                table[r ^ core, c] = ((r // n_col ^ group) * n_col + (c ^ offset) ^ land, c)
        targets = set(table.values())
        for r, c in devices:
            if (r ^ c) & 1 == 0:
                for taker in (r, r ^ 1):
                    for giver in (taker ^ 1, taker) if core else (taker ^ 1,):
                        if (giver, c) not in table and (taker, c) not in targets:
                            table[giver, c] = (taker, c)
                            targets.add((taker, c))
        return [(r * n_col + c, pr * n_col + pc) for (r, c), (pr, pc) in table.items()]

    offsets = list(range(0, n_col, 2))
    sibling = core_swap(lower_old)
    own_parts = [lower_old, sibling]
    for o in offsets[1:]:
        part = permute(lower_old, spread(0, o, 0))
        own_parts += [part, core_swap(part)]
    far = {}
    for g in range(1, n_high):
        far[g, 0] = permute(sibling, spread(g, 0, 1))
    for g in range(1, n_high):
        for o in offsets[1:]:
            far[g, o] = permute(lower_old, spread(g, o, 0))
    far_parts = []
    for g in range(1, n_high):
        for o in offsets:
            both = [far[g, o], core_swap(far[g, o])]
            far_parts += both

    w_shape = (2, slots * width, slots * width)
    ws = call(
        functools.partial(gather_kernel, n_high, slots),
        (pltpu.MemorySpace.HBM(w_shape, BF16),) * n_high,
        [SMEM, SMEM] + [ANY] * 4,
        [
            pltpu.VMEM((slots * n_cand, width, width), F32),
            pltpu.VMEM((n_high, *w_shape), BF16),
            pltpu.SMEM((kmax,), jnp.int32),
            pltpu.SMEM((kmax,), jnp.int32),
            pltpu.VMEM((DEPTH, width, width), BF16),
            pltpu.SMEM(inverse_rows.shape, jnp.int32),
            pltpu.SMEM(inverse_cols.shape, jnp.int32),
            pltpu.SMEM(panel_rows.shape, jnp.int32),
            pltpu.SemaphoreType.DMA((DEPTH,)),
            pltpu.SemaphoreType.DMA((n_high,)),
            pltpu.SemaphoreType.DMA((3,)),
        ],
        flops=block * 16,
        moved=16 * block * 2 + 16 * n_cand * slots * block,
        limit=6 + (slots * n_cand * 8 * block + DEPTH * 2 * block) // 2**20,
    )(
        me,
        inverse_count,
        *[
            pltpu.with_memory_space_constraint(value, pltpu.MemorySpace.HBM)
            for value in (inverse_rows, inverse_cols, panel_rows, blocks)
        ],
    )
    p_shape = (t_count, slots * width, width)
    p_own, old_t = call(
        own_kernel,
        (
            jax.ShapeDtypeStruct(p_shape, F32),
            jax.ShapeDtypeStruct((t_count, width, slots * width), BF16),
        ),
        [SMEM, ANY, VMEM] + [ANY] * len(own_parts),
        [
            pltpu.VMEM(w_shape, BF16),
            pltpu.VMEM(p_shape, BF16),
            pltpu.SemaphoreType.DMA,
            pltpu.SemaphoreType.DMA((t_count, slots)),
        ],
        flops=4 * block * width * slots * slots * t_count,
        moved=8 * block * t_count * slots,
        limit=12,
    )(
        where,
        pltpu.with_memory_space_constraint(ws[0], pltpu.MemorySpace.HBM),
        lower_old,
        *own_parts,
    )

    share = width // n_col
    n_blocks = t_count * (t_count + 1) // 2
    half = n_blocks * width // 2
    piece = half // n_plane
    u_shape = (n_col // 2, t_count, slots, share, width)
    u_keep, u_send, g_keep, g_send = call(
        functools.partial(main_kernel, n_high, n_col),
        (
            jax.ShapeDtypeStruct(u_shape, F32),
            jax.ShapeDtypeStruct(u_shape, BF16),
            jax.ShapeDtypeStruct((half, width), F32),
            jax.ShapeDtypeStruct((half, width), BF16),
        ),
        [SMEM, VMEM, VMEM, VMEM] + [VMEM] * (n_high - 1) + [ANY] * len(far_parts),
        [
            pltpu.VMEM((n_high - 1, t_count, slots * width, width), BF16),
            pltpu.VMEM((t_count, slots * width, width), F32),
            pltpu.VMEM((n_blocks * width, width), F32),
            pltpu.SemaphoreType.DMA((n_high - 1, t_count, slots)),
        ],
        flops=2 * block * width * slots * t_count * (2 * n_cand + 4),
        moved=4 * block * t_count * n_cand,
        limit=12 + 2 * n_high,
    )(where, p_own, old_t, lower_new, *ws[1:], *far_parts)

    def step(index):
        return pairs(
            anyone, lambda r, c: (r, c ^ 1 << (index if r & 1 == 0 else col_bits - 1 - index))
        )

    def halve(position, keep, received):
        shape = (keep.shape[0] // 2, *keep.shape[1:])
        return call(
            functools.partial(halving_kernel, position),
            (jax.ShapeDtypeStruct(shape, F32), jax.ShapeDtypeStruct(shape, BF16)),
            [SMEM, VMEM, VMEM],
            flops=keep.size,
            moved=keep.size * 6,
        )(where, keep, received)

    def add(dtype, values):
        return call(
            add_kernel,
            jax.ShapeDtypeStruct(values[0].shape, dtype),
            [VMEM] * len(values),
            flops=len(values) * values[0].size,
            moved=values[0].size * 2 * len(values),
        )(*values)

    keep = g_keep.reshape(n_plane, piece, width)
    received = core_swap(g_send)
    u_received = permute(u_send, step(0))
    shape = (piece, width)
    own, *sends = call(
        split_kernel,
        (jax.ShapeDtypeStruct(shape, F32), *[jax.ShapeDtypeStruct(shape, BF16)] * (n_plane - 1)),
        [SMEM, VMEM, VMEM],
        flops=half * width,
        moved=half * width * 8,
    )(where, keep, received.reshape(keep.shape))
    arrived = [
        permute(send, pairs(anyone, lambda r, c: (r ^ 2 * (m + 1), c)))
        for m, send in enumerate(sends)
    ]
    in_plane = add(BF16, [own, *arrived])
    level = [in_plane] + [
        permute(in_plane, pairs(anyone, lambda r, c: (r, c ^ m))) for m in range(1, n_col)
    ]
    for i in range(1, col_bits):
        u_keep, u_send = halve(5 + i - 1, u_keep, u_received)
        u_received = permute(u_send, step(i))
    total = add(BF16, level)
    pieces = [total] + [
        permute(total, pairs(anyone, lambda r, c: (r ^ 2 * m, c))) for m in range(1, n_plane)
    ]
    pieces += [core_swap(value) for value in pieces]
    supernode_inverse = call(
        final_kernel,
        pltpu.MemorySpace.HBM((t_count, t_count, width, width), F32),
        [SMEM] + [VMEM] * (2 + len(pieces)),
        [
            pltpu.VMEM((n_blocks * width, width), BF16),
            pltpu.VMEM((t_count, t_count, width, width), F32),
            pltpu.VMEM((width, width), F32),
            pltpu.SemaphoreType.DMA((t_count, t_count)),
        ],
        flops=2 * block * width * 16,
        moved=block * t_count * t_count * 6,
    )(where, lower_new, diag_inverse, *pieces)
    panel_inverse = add(BF16, [u_keep, u_received])[0]
    return (panel_inverse, supernode_inverse)


def solution(mesh):
    placed = (
        P("row", "col", None, None),
        P("row", "col"),
        P("row", "col"),
        P("row", "col"),
        P(),
        P(None, "row", None, None),
        P(),
        P(),
    )
    return jax.shard_map(
        per_device,
        mesh=mesh,
        in_specs=placed,
        out_specs=(P(None, "row", "col", None), P()),
        check_vma=False,
    )
```

```python
import functools

import jax
import jax.numpy as jnp
from jax import lax
from jax.experimental import pallas as pl
from jax.experimental.pallas import tpu as pltpu
from jax.sharding import PartitionSpec as P


BF16 = jnp.bfloat16
F32 = jnp.float32
VMEM = pl.BlockSpec(memory_space=pltpu.VMEM)
ANY = pl.BlockSpec(memory_space=pl.ANY)
SMEM = pl.BlockSpec(memory_space=pltpu.SMEM)
DEPTH = 8


def permute(value, pairs):
    return lax.ppermute(value, ("row", "col"), pairs)


def gather_kernel(groups, slots, me, count, rows_in, cols_in, panel_in, blocks, *refs):
    w_outs = refs[:groups]
    acc, w, order, code, buf, rows_ref, cols_ref, panel, sem, out_sem, in_sem = refs[groups:]
    width = buf.shape[-1]
    n_cand = groups * slots
    row_me = me[0]
    tables = ((rows_in, rows_ref), (cols_in, cols_ref), (panel_in, panel))
    brought = [pltpu.make_async_copy(*pair, in_sem.at[i]) for i, pair in enumerate(tables)]
    for copy in brought:
        copy.start()
    acc[...] = jnp.zeros_like(acc)
    for copy in brought:
        copy.wait()
    own = [panel[row_me * slots + s] for s in range(slots)]
    cand = [panel[me[1 + g] * slots + s] for g in range(groups) for s in range(slots)]
    step_size = 8 if rows_ref.shape[1] % 8 == 0 else 1

    def scan(step, n):
        for u in range(step_size):
            k = step * step_size + u
            row, col = rows_ref[0, k], cols_ref[0, k]
            where = jnp.int32(-1)
            for p in range(n_cand):
                where = jnp.where(col == cand[p], p, where)
            slot = jnp.int32(-1)
            for s in range(slots):
                slot = jnp.where(row == own[s], s, slot)
            order[n] = k
            code[n] = slot * n_cand + where
            used = (where >= 0) & (slot >= 0) & (k < count[0, 0])
            n = n + used.astype(jnp.int32)
        return n

    n_steps = (count[0, 0] + step_size - 1) // step_size
    n_used = lax.fori_loop(0, n_steps, scan, jnp.int32(0))

    def fetch(i):
        slot = lax.rem(i, DEPTH)
        return pltpu.make_async_copy(blocks.at[order[i]], buf.at[slot], sem.at[slot])

    for i in range(DEPTH):

        @pl.when(i < n_used)
        def _():
            fetch(jnp.int32(i)).start()

    def step(i, carry):
        fetch(i).wait()
        target = code[i]
        slot = lax.rem(i, DEPTH)
        acc[target] += buf[slot].astype(F32)

        @pl.when(i + DEPTH < n_used)
        def _():
            fetch(i + DEPTH).start()

        return carry

    lax.fori_loop(0, n_used, step, 0)
    for g in range(groups):
        for s in range(slots):
            for p in range(slots):
                rows = pl.ds(s * width, width)
                cols = pl.ds(p * width, width)
                value = acc[s * n_cand + g * slots + p]
                high = value.astype(BF16)
                w[g, 0, rows, cols] = high
                w[g, 1, rows, cols] = (value - high.astype(F32)).astype(BF16)
        pltpu.make_async_copy(w.at[g], w_outs[g], out_sem.at[g]).start()
    for g in range(groups):
        pltpu.make_async_copy(w.at[g], w_outs[g], out_sem.at[g]).wait()


def fill(where, options, lo, sems):
    count, slots, width = options[0].shape[:3]

    def copies(part, t):
        return [
            pltpu.make_async_copy(
                part.at[t, p], lo.at[t, pl.ds(p * width, width), :], sems.at[t, p]
            )
            for p in range(slots)
        ]

    for case, part in enumerate(options):

        @pl.when(where[0] == case)
        def _():
            for t in range(count):
                for copy in copies(part, t):
                    copy.start()

    def wait(t):
        for copy in copies(options[0], t):
            copy.wait()

    return wait


def stacked_dot(w, panel):
    both = jnp.dot(w.reshape(-1, w.shape[-1]), panel, preferred_element_type=F32)
    return both[: w.shape[1]] + both[w.shape[1] :]


def own_kernel(where, w_in, old, new, *refs):
    options, (p_out, old_out, new_out, w, lo, w_sem, sems) = refs[:-7], refs[-7:]
    w_copy = pltpu.make_async_copy(w_in, w, w_sem)
    w_copy.start()
    wait = fill(where, options, lo, sems)
    for t in range(lo.shape[0]):
        old_out[t] = old[t].reshape(lo.shape[1:]).T
        for s in range(t):
            new_out[t * (t - 1) // 2 + s] = new[t, s].T
    w_copy.wait()
    for t in range(lo.shape[0]):
        wait(t)
        p_out[t] = stacked_dot(w[...], lo[t])


def piece_index(core, value, j, count):
    return jnp.where(core == 0, 2 * j + value, value * count + j)


def main_kernel(n_high, n_col, where, p_own, old_t, new, *refs):
    t_count = new.shape[0]
    width = new.shape[-1]
    slots = old_t.shape[-1] // width
    n_far = n_high - 1
    w_ins, parts = refs[:n_far], refs[n_far:-7]
    u_keep, u_send, g_all, g_send, lo, u_all, sems = refs[-7:]
    cases = len(parts) // max(n_far, 1)
    waits = [
        fill(where, parts[g * cases : (g + 1) * cases], lo.at[g], sems.at[g]) for g in range(n_far)
    ]
    for t in range(t_count):
        for wait in waits:
            wait(t)
    share = width // n_col
    count = n_col // 2
    totals = [
        p_own[t] + sum(stacked_dot(w_ins[g][...], lo[g, t]) for g in range(n_far))
        for t in range(t_count)
    ]
    for s in range(t_count):
        u_all[s] = -totals[s]
        panel = (-totals[s]).astype(BF16)
        for value, out in ((where[4], u_keep), (1 - where[4], u_send)):
            for j in range(count):
                start = piece_index(where[1], value, j, count) * share
                for p in range(slots):
                    window = pl.ds(pl.multiple_of(p * width + start, 16), share)
                    out[j, s, p] = u_all[s, window, :].astype(out.dtype)
        for t in range(s + 1, t_count):
            totals[t] += jnp.dot(panel, new[t, s], preferred_element_type=F32)
        rest = old_t[s:].reshape(-1, old_t.shape[-1])
        crossed = jnp.dot(rest, panel, preferred_element_type=F32)
        for t in range(s, t_count):
            g_all[pl.ds((t * (t + 1) // 2 + s) * width, width), :] = crossed[
                (t - s) * width : (t - s + 1) * width
            ]
    half = g_send.shape[0]
    g_send[...] = g_all[pl.ds(pl.multiple_of((1 - where[1]) * half, 16), half), :].astype(BF16)


def halving_kernel(bit, where, keep, received, keep_out, send_out):
    count = keep_out.shape[0]
    for value, out in ((where[bit], keep_out), (1 - where[bit], send_out)):
        for j in range(count):
            index = piece_index(where[1], value, j, count)
            out[j] = (keep[index] + received[index].astype(F32)).astype(out.dtype)


def split_kernel(where, keep, received, own, *sends):
    def piece(m):
        index = where[3] ^ m
        kept = keep[where[1] * received.shape[0] + index]
        return kept + received[index].astype(F32)

    own[...] = piece(0)
    for m, send in enumerate(sends):
        send[...] = piece(m + 1).astype(BF16)


def tree(values):
    while len(values) > 1:
        values = [a + b for a, b in zip(values[::2], values[1::2])]
    return values[0]


def add_kernel(*refs):
    out = refs[-1]
    out[...] = tree([ref[...].astype(F32) for ref in refs[:-1]]).astype(out.dtype)


def wide_dot(left, right, dims):
    wide = left if left.dtype == F32 else right
    high = wide.astype(BF16)
    low = (wide - high.astype(F32)).astype(BF16)
    if left.dtype == F32:
        axis = 1 - dims[0][0]
        both = lax.dot_general(
            jnp.concatenate([high, low], axis),
            right,
            (dims, ((), ())),
            preferred_element_type=F32,
        )
        return both[: left.shape[axis]] + both[left.shape[axis] :]
    parts = [
        lax.dot_general(left, part, (dims, ((), ())), preferred_element_type=F32)
        for part in (high, low)
    ]
    return parts[0] + parts[1]


def final_kernel(where, new, new_t, diag, *refs):
    pieces, (out, g_all, y, zero, sems) = refs[:-5], refs[-5:]
    t_count = new.shape[0]
    width = new.shape[-1]
    n_plane = len(pieces) // 2
    rows = pieces[0].shape[0]
    for i, piece in enumerate(pieces):
        core, chip = where[1] ^ i // n_plane, where[3] ^ i % n_plane
        place = (core * n_plane + chip) * rows
        g_all[pl.ds(pl.multiple_of(place, 16), rows), :] = piece[...]

    def g(t, s):
        index = t * (t + 1) // 2 + s
        value = g_all[pl.ds(index * width, width), :]
        return (value if s == t else value.T).astype(F32)

    def give(source, t, s):
        copy = pltpu.make_async_copy(source, out.at[t, s], sems.at[t, s])
        copy.start()
        sent.append(copy)

    sent = []
    zero[...] = jnp.zeros_like(zero)
    for t in range(t_count):
        for s in range(t + 1, t_count):
            give(zero, t, s)
    blocks = {}
    for t in range(t_count):
        for s in range(t):
            crossed = g(t, s)
            for u in range(t):
                if u >= s:
                    crossed += wide_dot(blocks[u, s], new[t, u], ((1,), (0,)))
                else:
                    crossed += wide_dot(blocks[s, u], new[t, u], ((0,), (0,)))
            blocks[t, s] = -crossed
            y[t, s] = blocks[t, s]
            give(y.at[t, s], t, s)
        diagonal = diag[t] - g(t, t)
        for s in range(t):
            diagonal -= wide_dot(new_t[t * (t - 1) // 2 + s], blocks[t, s], ((1,), (0,)))
        blocks[t, t] = diagonal
        y[t, t] = diagonal
        give(y.at[t, t], t, t)
    for copy in sent:
        copy.wait()


def call(kernel, shapes, in_specs, scratch=(), flops=0, moved=0, limit=8):
    def place(shape):
        if not isinstance(shape, jax.ShapeDtypeStruct):
            return ANY
        return SMEM if shape.dtype == jnp.int32 else VMEM

    return pl.pallas_call(
        kernel,
        out_shape=shapes,
        in_specs=in_specs,
        out_specs=tuple(map(place, shapes)) if isinstance(shapes, tuple) else place(shapes),
        scratch_shapes=list(scratch),
        cost_estimate=pl.CostEstimate(flops=flops, bytes_accessed=moved, transcendentals=0),
        compiler_params=pltpu.CompilerParams(vmem_limit_bytes=limit << 20),
    )


def per_device(
    inverse_blocks,
    inverse_rows,
    inverse_cols,
    inverse_count,
    panel_rows,
    lower_old,
    lower_new,
    diag_inverse,
):
    blocks = inverse_blocks[0]
    kmax = blocks.shape[0]
    width = blocks.shape[-1]
    t_count, slots = lower_old.shape[:2]
    n_row = lax.axis_size("row")
    n_col = lax.axis_size("col")
    row_me = lax.axis_index("row")
    col_me = lax.axis_index("col")
    devices = [(r, c) for r in range(n_row) for c in range(n_col)]
    n_high = n_row // n_col
    n_plane = n_row // 2

    def pairs(active, partner):
        return [
            (r * n_col + c, pr * n_col + pc)
            for r, c in devices
            if active(r, c)
            for pr, pc in [partner(r, c)]
        ]

    high_me = row_me // n_col
    groups = [((high_me ^ g) * n_col + col_me) for g in range(n_high)]
    n_cand = n_high * slots
    me = jnp.stack([row_me, *groups]).astype(jnp.int32)
    source = (row_me ^ col_me) & (n_col - 1)
    core_me = row_me & 1
    chip_me = row_me >> 1
    col_bits = n_col.bit_length() - 1

    def bit_of(value, bits, i):
        return jnp.where(core_me == 0, value >> i, value >> bits - 1 - i) & 1

    where = jnp.stack(
        [source, core_me, col_me, chip_me] + [bit_of(col_me, col_bits, i) for i in range(col_bits)]
    ).astype(jnp.int32)

    block = width * width
    anyone = lambda r, c: True

    def core_swap(value):
        return permute(value, pairs(anyone, lambda r, c: (r ^ 1, c)))

    def spread(group, offset, core, land=0):
        table = {}
        for r, c in devices:
            if r % n_col == c:
                table[r ^ core, c] = ((r // n_col ^ group) * n_col + (c ^ offset) ^ land, c)
        targets = set(table.values())
        for r, c in devices:
            if (r ^ c) & 1 == 0:
                for taker in (r, r ^ 1):
                    for giver in (taker ^ 1, taker) if core else (taker ^ 1,):
                        if (giver, c) not in table and (taker, c) not in targets:
                            table[giver, c] = (taker, c)
                            targets.add((taker, c))
        return [(r * n_col + c, pr * n_col + pc) for (r, c), (pr, pc) in table.items()]

    offsets = list(range(0, n_col, 2))
    sibling = core_swap(lower_old)
    own_parts = [lower_old, sibling]
    for o in offsets[1:]:
        part = permute(lower_old, spread(0, o, 0))
        own_parts += [part, core_swap(part)]
    far = {}
    for g in range(1, n_high):
        far[g, 0] = permute(lower_old, spread(g, 0, 0, 1))
    for g in range(1, n_high):
        for o in offsets[1:]:
            far[g, o] = permute(sibling, spread(g, o, 1))
    far_parts = []
    for g in range(1, n_high):
        for o in offsets:
            both = [far[g, o], core_swap(far[g, o])]
            far_parts += both if o else both[::-1]

    w_shape = (2, slots * width, slots * width)
    ws = call(
        functools.partial(gather_kernel, n_high, slots),
        (pltpu.MemorySpace.HBM(w_shape, BF16),) * n_high,
        [SMEM, SMEM] + [ANY] * 4,
        [
            pltpu.VMEM((slots * n_cand, width, width), F32),
            pltpu.VMEM((n_high, *w_shape), BF16),
            pltpu.SMEM((kmax,), jnp.int32),
            pltpu.SMEM((kmax,), jnp.int32),
            pltpu.VMEM((DEPTH, width, width), BF16),
            pltpu.SMEM(inverse_rows.shape, jnp.int32),
            pltpu.SMEM(inverse_cols.shape, jnp.int32),
            pltpu.SMEM(panel_rows.shape, jnp.int32),
            pltpu.SemaphoreType.DMA((DEPTH,)),
            pltpu.SemaphoreType.DMA((n_high,)),
            pltpu.SemaphoreType.DMA((3,)),
        ],
        flops=block * 16,
        moved=16 * block * 2 + 16 * n_cand * slots * block,
        limit=6 + (slots * n_cand * 8 * block + DEPTH * 2 * block) // 2**20,
    )(
        me,
        inverse_count,
        *[
            pltpu.with_memory_space_constraint(value, pltpu.MemorySpace.HBM)
            for value in (inverse_rows, inverse_cols, panel_rows, blocks)
        ],
    )
    p_shape = (t_count, slots * width, width)
    p_own, old_t, new_t = call(
        own_kernel,
        (
            jax.ShapeDtypeStruct(p_shape, F32),
            jax.ShapeDtypeStruct((t_count, width, slots * width), BF16),
            jax.ShapeDtypeStruct((max(t_count * (t_count - 1) // 2, 1), width, width), BF16),
        ),
        [SMEM, ANY, VMEM, VMEM] + [ANY] * len(own_parts),
        [
            pltpu.VMEM(w_shape, BF16),
            pltpu.VMEM(p_shape, BF16),
            pltpu.SemaphoreType.DMA,
            pltpu.SemaphoreType.DMA((t_count, slots)),
        ],
        flops=4 * block * width * slots * slots * t_count,
        moved=8 * block * t_count * slots,
        limit=12,
    )(
        where,
        pltpu.with_memory_space_constraint(ws[0], pltpu.MemorySpace.HBM),
        lower_old,
        lower_new,
        *own_parts,
    )

    share = width // n_col
    n_blocks = t_count * (t_count + 1) // 2
    half = n_blocks * width // 2
    piece = half // n_plane
    u_shape = (n_col // 2, t_count, slots, share, width)
    u_keep, u_send, g_all, g_send = call(
        functools.partial(main_kernel, n_high, n_col),
        (
            jax.ShapeDtypeStruct(u_shape, F32),
            jax.ShapeDtypeStruct(u_shape, BF16),
            jax.ShapeDtypeStruct((2 * half, width), F32),
            jax.ShapeDtypeStruct((half, width), BF16),
        ),
        [SMEM, VMEM, VMEM, VMEM] + [VMEM] * (n_high - 1) + [ANY] * len(far_parts),
        [
            pltpu.VMEM((n_high - 1, t_count, slots * width, width), BF16),
            pltpu.VMEM((t_count, slots * width, width), F32),
            pltpu.SemaphoreType.DMA((n_high - 1, t_count, slots)),
        ],
        flops=2 * block * width * slots * t_count * (2 * n_cand + 4),
        moved=4 * block * t_count * n_cand,
        limit=12 + 2 * n_high,
    )(where, p_own, old_t, lower_new, *ws[1:], *far_parts)

    def step(index):
        return pairs(
            anyone, lambda r, c: (r, c ^ 1 << (index if r & 1 == 0 else col_bits - 1 - index))
        )

    def halve(position, keep, received):
        shape = (keep.shape[0] // 2, *keep.shape[1:])
        return call(
            functools.partial(halving_kernel, position),
            (jax.ShapeDtypeStruct(shape, F32), jax.ShapeDtypeStruct(shape, BF16)),
            [SMEM, VMEM, VMEM],
            flops=keep.size,
            moved=keep.size * 6,
        )(where, keep, received)

    def add(dtype, values):
        return call(
            add_kernel,
            jax.ShapeDtypeStruct(values[0].shape, dtype),
            [VMEM] * len(values),
            flops=len(values) * values[0].size,
            moved=values[0].size * 2 * len(values),
        )(*values)

    keep = g_all.reshape(2 * n_plane, piece, width)
    received = core_swap(g_send)
    u_received = permute(u_send, step(0))
    shape = (piece, width)
    own, *sends = call(
        split_kernel,
        (jax.ShapeDtypeStruct(shape, F32), *[jax.ShapeDtypeStruct(shape, BF16)] * (n_plane - 1)),
        [SMEM, VMEM, VMEM],
        flops=half * width,
        moved=half * width * 8,
    )(where, keep, received.reshape(n_plane, piece, width))
    arrived = [
        permute(send, pairs(anyone, lambda r, c: (r ^ 2 * (m + 1), c)))
        for m, send in enumerate(sends)
    ]
    in_plane = add(BF16, [own, *arrived])
    level = [in_plane] + [
        permute(in_plane, pairs(anyone, lambda r, c: (r, c ^ m))) for m in range(1, n_col)
    ]
    for i in range(1, col_bits):
        u_keep, u_send = halve(5 + i - 1, u_keep, u_received)
        u_received = permute(u_send, step(i))
    total = add(BF16, level)
    pieces = [total] + [
        permute(total, pairs(anyone, lambda r, c: (r ^ 2 * m, c))) for m in range(1, n_plane)
    ]
    pieces += [core_swap(value) for value in pieces]
    supernode_inverse = call(
        final_kernel,
        pltpu.MemorySpace.HBM((t_count, t_count, width, width), F32),
        [SMEM] + [VMEM] * (3 + len(pieces)),
        [
            pltpu.VMEM((n_blocks * width, width), BF16),
            pltpu.VMEM((t_count, t_count, width, width), F32),
            pltpu.VMEM((width, width), F32),
            pltpu.SemaphoreType.DMA((t_count, t_count)),
        ],
        flops=2 * block * width * 16,
        moved=block * t_count * t_count * 6,
    )(where, lower_new, new_t, diag_inverse, *pieces)
    panel_inverse = add(BF16, [u_keep, u_received])[0]
    return (panel_inverse, supernode_inverse)


def solution(mesh):
    placed = (
        P("row", "col", None, None),
        P("row", "col"),
        P("row", "col"),
        P("row", "col"),
        P(),
        P(None, "row", None, None),
        P(),
        P(),
    )
    return jax.shard_map(
        per_device,
        mesh=mesh,
        in_specs=placed,
        out_specs=(P(None, "row", "col", None), P()),
        check_vma=False,
    )
```

```python
import functools

import jax
import jax.numpy as jnp
from jax import lax
from jax.experimental import pallas as pl
from jax.experimental.pallas import tpu as pltpu
from jax.sharding import PartitionSpec as P


BF16 = jnp.bfloat16
F32 = jnp.float32
VMEM = pl.BlockSpec(memory_space=pltpu.VMEM)
ANY = pl.BlockSpec(memory_space=pl.ANY)
SMEM = pl.BlockSpec(memory_space=pltpu.SMEM)
DEPTH = 16


def permute(value, pairs):
    return lax.ppermute(value, ("row", "col"), pairs)


def gather_kernel(groups, slots, me, count, rows_in, cols_in, panel_in, blocks, *refs):
    w_outs = refs[:groups]
    acc, w, order, code, buf, rows_ref, cols_ref, panel, sem, out_sem, in_sem = refs[groups:]
    width = buf.shape[-1]
    n_cand = groups * slots
    row_me = me[0]
    tables = ((rows_in, rows_ref), (cols_in, cols_ref), (panel_in, panel))
    brought = [pltpu.make_async_copy(*pair, in_sem.at[i]) for i, pair in enumerate(tables)]
    for copy in brought:
        copy.start()
    acc[...] = jnp.zeros_like(acc)
    for copy in brought:
        copy.wait()
    own = [panel[row_me * slots + s] for s in range(slots)]
    cand = [panel[me[1 + g] * slots + s] for g in range(groups) for s in range(slots)]
    step_size = 8 if rows_ref.shape[1] % 8 == 0 else 1

    def scan(step, n):
        for u in range(step_size):
            k = step * step_size + u
            row, col = rows_ref[0, k], cols_ref[0, k]
            where = jnp.int32(-1)
            for p in range(n_cand):
                where = jnp.where(col == cand[p], p, where)
            slot = jnp.int32(0)
            for s in range(1, slots):
                slot = jnp.where(row == own[s], s, slot)
            order[n] = k
            code[n] = slot * n_cand + where
            used = (where >= 0) & (k < count[0, 0])
            n = n + used.astype(jnp.int32)
        return n

    n_steps = (count[0, 0] + step_size - 1) // step_size
    n_used = lax.fori_loop(0, n_steps, scan, jnp.int32(0))

    def fetch(i):
        slot = lax.rem(i, DEPTH)
        return pltpu.make_async_copy(blocks.at[order[i]], buf.at[slot], sem.at[slot])

    for i in range(DEPTH):

        @pl.when(i < n_used)
        def _():
            fetch(jnp.int32(i)).start()

    def step(i, carry):
        fetch(i).wait()
        target = code[i]
        slot = lax.rem(i, DEPTH)
        acc[target] += buf[slot].astype(F32)

        @pl.when(i + DEPTH < n_used)
        def _():
            fetch(i + DEPTH).start()

        return carry

    lax.fori_loop(0, n_used, step, 0)
    for g in range(groups):
        for s in range(slots):
            for p in range(slots):
                rows = pl.ds(s * width, width)
                cols = pl.ds(p * width, width)
                value = acc[s * n_cand + g * slots + p]
                high = value.astype(BF16)
                w[g, 0, rows, cols] = high
                w[g, 1, rows, cols] = (value - high.astype(F32)).astype(BF16)
        pltpu.make_async_copy(w.at[g], w_outs[g], out_sem.at[g]).start()
    for g in range(groups):
        pltpu.make_async_copy(w.at[g], w_outs[g], out_sem.at[g]).wait()


def fill(where, options, lo, sems):
    count, slots, width = options[0].shape[:3]

    def copies(part, t):
        return [
            pltpu.make_async_copy(
                part.at[t, p], lo.at[t, pl.ds(p * width, width), :], sems.at[t, p]
            )
            for p in range(slots)
        ]

    for case, part in enumerate(options):

        @pl.when(where[0] == case)
        def _():
            for t in range(count):
                for copy in copies(part, t):
                    copy.start()

    def wait(t):
        for copy in copies(options[0], t):
            copy.wait()

    return wait


def stacked_dot(w, panel):
    both = jnp.dot(w.reshape(-1, w.shape[-1]), panel, preferred_element_type=F32)
    return both[: w.shape[1]] + both[w.shape[1] :]


def own_kernel(where, w_in, old, *refs):
    options, (p_out, old_out, w, lo, w_sem, sems) = refs[:-6], refs[-6:]
    w_copy = pltpu.make_async_copy(w_in, w, w_sem)
    w_copy.start()
    wait = fill(where, options, lo, sems)
    for t in range(lo.shape[0]):
        old_out[t] = old[t].reshape(lo.shape[1:]).T
    w_copy.wait()
    for t in range(lo.shape[0]):
        wait(t)
        p_out[t] = stacked_dot(w[...], lo[t])


def piece_index(core, value, j, count):
    return jnp.where(core == 0, 2 * j + value, value * count + j)


def main_kernel(n_high, n_col, where, p_own, old_t, new, *refs):
    t_count = new.shape[0]
    width = new.shape[-1]
    slots = old_t.shape[-1] // width
    n_far = n_high - 1
    w_ins, parts = refs[:n_far], refs[n_far:-8]
    u_keep, u_send, g_keep, g_send, lo, u_all, g_all, sems = refs[-8:]
    cases = len(parts) // max(n_far, 1)
    waits = [
        fill(where, parts[g * cases : (g + 1) * cases], lo.at[g], sems.at[g]) for g in range(n_far)
    ]
    for t in range(t_count):
        for wait in waits:
            wait(t)
    totals = [
        p_own[t] + sum(stacked_dot(w_ins[g][...], lo[g, t]) for g in range(n_far))
        for t in range(t_count)
    ]
    for s in range(t_count):
        u_all[s] = -totals[s]
        panel = (-totals[s]).astype(BF16)
        for t in range(s + 1, t_count):
            totals[t] += jnp.dot(panel, new[t, s], preferred_element_type=F32)
        rest = old_t[s:].reshape(-1, old_t.shape[-1])
        crossed = jnp.dot(rest, panel, preferred_element_type=F32)
        for t in range(s, t_count):
            g_all[pl.ds((t * (t + 1) // 2 + s) * width, width), :] = crossed[
                (t - s) * width : (t - s + 1) * width
            ]
    half = g_keep.shape[0]
    g_keep[...] = g_all[pl.ds(pl.multiple_of(where[1] * half, 16), half), :]
    g_send[...] = g_all[pl.ds(pl.multiple_of((1 - where[1]) * half, 16), half), :].astype(BF16)
    share = width // n_col
    count = n_col // 2
    for value, out in ((where[4], u_keep), (1 - where[4], u_send)):
        for j in range(count):
            start = piece_index(where[1], value, j, count) * share
            for t in range(t_count):
                for s in range(slots):
                    window = pl.ds(pl.multiple_of(s * width + start, 16), share)
                    out[j, t, s] = u_all[t, window, :].astype(out.dtype)


def halving_kernel(bit, where, keep, received, keep_out, send_out):
    count = keep_out.shape[0]
    for value, out in ((where[bit], keep_out), (1 - where[bit], send_out)):
        for j in range(count):
            index = piece_index(where[1], value, j, count)
            out[j] = (keep[index] + received[index].astype(F32)).astype(out.dtype)


def split_kernel(where, keep, received, own, *sends):
    def piece(m):
        index = where[3] ^ m
        return keep[index] + received[index].astype(F32)

    own[...] = piece(0)
    for m, send in enumerate(sends):
        send[...] = piece(m + 1).astype(BF16)


def tree(values):
    while len(values) > 1:
        values = [a + b for a, b in zip(values[::2], values[1::2])]
    return values[0]


def add_kernel(*refs):
    out = refs[-1]
    out[...] = tree([ref[...].astype(F32) for ref in refs[:-1]]).astype(out.dtype)


def wide_dot(left, right, dims):
    wide = left if left.dtype == F32 else right
    high = wide.astype(BF16)
    low = (wide - high.astype(F32)).astype(BF16)
    if left.dtype == F32:
        axis = 1 - dims[0][0]
        both = lax.dot_general(
            jnp.concatenate([high, low], axis),
            right,
            (dims, ((), ())),
            preferred_element_type=F32,
        )
        return both[: left.shape[axis]] + both[left.shape[axis] :]
    parts = [
        lax.dot_general(left, part, (dims, ((), ())), preferred_element_type=F32)
        for part in (high, low)
    ]
    return parts[0] + parts[1]


def final_kernel(where, new, diag, *refs):
    pieces, (out, g_all, y, zero, sems) = refs[:-5], refs[-5:]
    t_count = new.shape[0]
    width = new.shape[-1]
    n_plane = len(pieces) // 2
    rows = pieces[0].shape[0]
    for i, piece in enumerate(pieces):
        core, chip = where[1] ^ i // n_plane, where[3] ^ i % n_plane
        place = (core * n_plane + chip) * rows
        g_all[pl.ds(pl.multiple_of(place, 16), rows), :] = piece[...]

    def g(t, s):
        index = t * (t + 1) // 2 + s
        value = g_all[pl.ds(index * width, width), :]
        return (value if s == t else value.T).astype(F32)

    def give(source, t, s):
        copy = pltpu.make_async_copy(source, out.at[t, s], sems.at[t, s])
        copy.start()
        sent.append(copy)

    sent = []
    zero[...] = jnp.zeros_like(zero)
    for t in range(t_count):
        for s in range(t + 1, t_count):
            give(zero, t, s)
    blocks = {}
    for t in range(t_count):
        for s in range(t):
            crossed = g(t, s)
            for u in range(t):
                if u >= s:
                    crossed += wide_dot(blocks[u, s], new[t, u], ((1,), (0,)))
                else:
                    crossed += wide_dot(blocks[s, u], new[t, u], ((0,), (0,)))
            blocks[t, s] = -crossed
            y[t, s] = blocks[t, s]
            give(y.at[t, s], t, s)
        diagonal = diag[t] - g(t, t)
        for s in range(t):
            diagonal -= wide_dot(new[t, s], blocks[t, s], ((0,), (0,)))
        blocks[t, t] = diagonal
        y[t, t] = diagonal
        give(y.at[t, t], t, t)
    for copy in sent:
        copy.wait()


def call(kernel, shapes, in_specs, scratch=(), flops=0, moved=0, limit=8):
    def place(shape):
        if not isinstance(shape, jax.ShapeDtypeStruct):
            return ANY
        return SMEM if shape.dtype == jnp.int32 else VMEM

    return pl.pallas_call(
        kernel,
        out_shape=shapes,
        in_specs=in_specs,
        out_specs=tuple(map(place, shapes)) if isinstance(shapes, tuple) else place(shapes),
        scratch_shapes=list(scratch),
        cost_estimate=pl.CostEstimate(flops=flops, bytes_accessed=moved, transcendentals=0),
        compiler_params=pltpu.CompilerParams(vmem_limit_bytes=limit << 20),
    )


def per_device(
    inverse_blocks,
    inverse_rows,
    inverse_cols,
    inverse_count,
    panel_rows,
    lower_old,
    lower_new,
    diag_inverse,
):
    blocks = inverse_blocks[0]
    kmax = blocks.shape[0]
    width = blocks.shape[-1]
    t_count, slots = lower_old.shape[:2]
    n_row = lax.axis_size("row")
    n_col = lax.axis_size("col")
    row_me = lax.axis_index("row")
    col_me = lax.axis_index("col")
    devices = [(r, c) for r in range(n_row) for c in range(n_col)]
    n_high = n_row // n_col
    n_plane = n_row // 2

    def pairs(active, partner):
        return [
            (r * n_col + c, pr * n_col + pc)
            for r, c in devices
            if active(r, c)
            for pr, pc in [partner(r, c)]
        ]

    high_me = row_me // n_col
    groups = [((high_me ^ g) * n_col + col_me) for g in range(n_high)]
    n_cand = n_high * slots
    me = jnp.stack([row_me, *groups]).astype(jnp.int32)
    source = (row_me ^ col_me) & (n_col - 1)
    core_me = row_me & 1
    chip_me = row_me >> 1
    col_bits = n_col.bit_length() - 1

    def bit_of(value, bits, i):
        return jnp.where(core_me == 0, value >> i, value >> bits - 1 - i) & 1

    where = jnp.stack(
        [source, core_me, col_me, chip_me] + [bit_of(col_me, col_bits, i) for i in range(col_bits)]
    ).astype(jnp.int32)

    block = width * width
    anyone = lambda r, c: True

    def core_swap(value):
        return permute(value, pairs(anyone, lambda r, c: (r ^ 1, c)))

    def spread(group, offset, core, land=0):
        table = {}
        for r, c in devices:
            if r % n_col == c:
                table[r ^ core, c] = ((r // n_col ^ group) * n_col + (c ^ offset) ^ land, c)
        targets = set(table.values())
        for r, c in devices:
            if (r ^ c) & 1 == 0:
                for taker in (r, r ^ 1):
                    for giver in (taker ^ 1, taker) if core else (taker ^ 1,):
                        if (giver, c) not in table and (taker, c) not in targets:
                            table[giver, c] = (taker, c)
                            targets.add((taker, c))
        return [(r * n_col + c, pr * n_col + pc) for (r, c), (pr, pc) in table.items()]

    offsets = list(range(0, n_col, 2))
    sibling = core_swap(lower_old)
    own_parts = [lower_old, sibling]
    for o in offsets[1:]:
        part = permute(lower_old, spread(0, o, 0))
        own_parts += [part, core_swap(part)]
    far = {}
    for g in range(1, n_high):
        far[g, 0] = permute(lower_old, spread(g, 0, 0, 1))
    for g in range(1, n_high):
        for o in offsets[1:]:
            far[g, o] = permute(sibling, spread(g, o, 1))
    far_parts = []
    for g in range(1, n_high):
        for o in offsets:
            both = [far[g, o], core_swap(far[g, o])]
            far_parts += both if o else both[::-1]

    w_shape = (2, slots * width, slots * width)
    ws = call(
        functools.partial(gather_kernel, n_high, slots),
        (pltpu.MemorySpace.HBM(w_shape, BF16),) * n_high,
        [SMEM, SMEM] + [ANY] * 4,
        [
            pltpu.VMEM((slots * n_cand, width, width), F32),
            pltpu.VMEM((n_high, *w_shape), BF16),
            pltpu.SMEM((kmax,), jnp.int32),
            pltpu.SMEM((kmax,), jnp.int32),
            pltpu.VMEM((DEPTH, width, width), BF16),
            pltpu.SMEM(inverse_rows.shape, jnp.int32),
            pltpu.SMEM(inverse_cols.shape, jnp.int32),
            pltpu.SMEM(panel_rows.shape, jnp.int32),
            pltpu.SemaphoreType.DMA((DEPTH,)),
            pltpu.SemaphoreType.DMA((n_high,)),
            pltpu.SemaphoreType.DMA((3,)),
        ],
        flops=block * 16,
        moved=16 * block * 2 + 16 * n_cand * slots * block,
        limit=6 + (slots * n_cand * 8 * block + DEPTH * 2 * block) // 2**20,
    )(
        me,
        inverse_count,
        *[
            pltpu.with_memory_space_constraint(value, pltpu.MemorySpace.HBM)
            for value in (inverse_rows, inverse_cols, panel_rows, blocks)
        ],
    )
    p_shape = (t_count, slots * width, width)
    p_own, old_t = call(
        own_kernel,
        (
            jax.ShapeDtypeStruct(p_shape, F32),
            jax.ShapeDtypeStruct((t_count, width, slots * width), BF16),
        ),
        [SMEM, ANY, VMEM] + [ANY] * len(own_parts),
        [
            pltpu.VMEM(w_shape, BF16),
            pltpu.VMEM(p_shape, BF16),
            pltpu.SemaphoreType.DMA,
            pltpu.SemaphoreType.DMA((t_count, slots)),
        ],
        flops=4 * block * width * slots * slots * t_count,
        moved=8 * block * t_count * slots,
        limit=12,
    )(
        where,
        pltpu.with_memory_space_constraint(ws[0], pltpu.MemorySpace.HBM),
        lower_old,
        *own_parts,
    )

    share = width // n_col
    n_blocks = t_count * (t_count + 1) // 2
    half = n_blocks * width // 2
    piece = half // n_plane
    u_shape = (n_col // 2, t_count, slots, share, width)
    u_keep, u_send, g_keep, g_send = call(
        functools.partial(main_kernel, n_high, n_col),
        (
            jax.ShapeDtypeStruct(u_shape, F32),
            jax.ShapeDtypeStruct(u_shape, BF16),
            jax.ShapeDtypeStruct((half, width), F32),
            jax.ShapeDtypeStruct((half, width), BF16),
        ),
        [SMEM, VMEM, VMEM, VMEM] + [VMEM] * (n_high - 1) + [ANY] * len(far_parts),
        [
            pltpu.VMEM((n_high - 1, t_count, slots * width, width), BF16),
            pltpu.VMEM((t_count, slots * width, width), F32),
            pltpu.VMEM((n_blocks * width, width), F32),
            pltpu.SemaphoreType.DMA((n_high - 1, t_count, slots)),
        ],
        flops=2 * block * width * slots * t_count * (2 * n_cand + 4),
        moved=4 * block * t_count * n_cand,
        limit=12 + 2 * n_high,
    )(where, p_own, old_t, lower_new, *ws[1:], *far_parts)

    def step(index):
        return pairs(
            anyone, lambda r, c: (r, c ^ 1 << (index if r & 1 == 0 else col_bits - 1 - index))
        )

    def halve(position, keep, received):
        shape = (keep.shape[0] // 2, *keep.shape[1:])
        return call(
            functools.partial(halving_kernel, position),
            (jax.ShapeDtypeStruct(shape, F32), jax.ShapeDtypeStruct(shape, BF16)),
            [SMEM, VMEM, VMEM],
            flops=keep.size,
            moved=keep.size * 6,
        )(where, keep, received)

    def add(dtype, values):
        return call(
            add_kernel,
            jax.ShapeDtypeStruct(values[0].shape, dtype),
            [VMEM] * len(values),
            flops=len(values) * values[0].size,
            moved=values[0].size * 2 * len(values),
        )(*values)

    keep = g_keep.reshape(n_plane, piece, width)
    received = core_swap(g_send)
    u_received = permute(u_send, step(0))
    shape = (piece, width)
    own, *sends = call(
        split_kernel,
        (jax.ShapeDtypeStruct(shape, F32), *[jax.ShapeDtypeStruct(shape, BF16)] * (n_plane - 1)),
        [SMEM, VMEM, VMEM],
        flops=half * width,
        moved=half * width * 8,
    )(where, keep, received.reshape(keep.shape))
    arrived = [
        permute(send, pairs(anyone, lambda r, c: (r ^ 2 * (m + 1), c)))
        for m, send in enumerate(sends)
    ]
    in_plane = add(BF16, [own, *arrived])
    level = [in_plane] + [
        permute(in_plane, pairs(anyone, lambda r, c: (r, c ^ m))) for m in range(1, n_col)
    ]
    for i in range(1, col_bits):
        u_keep, u_send = halve(5 + i - 1, u_keep, u_received)
        u_received = permute(u_send, step(i))
    total = add(BF16, level)
    pieces = [total] + [
        permute(total, pairs(anyone, lambda r, c: (r ^ 2 * m, c))) for m in range(1, n_plane)
    ]
    pieces += [core_swap(value) for value in pieces]
    supernode_inverse = call(
        final_kernel,
        pltpu.MemorySpace.HBM((t_count, t_count, width, width), F32),
        [SMEM] + [VMEM] * (2 + len(pieces)),
        [
            pltpu.VMEM((n_blocks * width, width), BF16),
            pltpu.VMEM((t_count, t_count, width, width), F32),
            pltpu.VMEM((width, width), F32),
            pltpu.SemaphoreType.DMA((t_count, t_count)),
        ],
        flops=2 * block * width * 16,
        moved=block * t_count * t_count * 6,
    )(where, lower_new, diag_inverse, *pieces)
    panel_inverse = add(BF16, [u_keep, u_received])[0]
    return (panel_inverse, supernode_inverse)


def solution(mesh):
    placed = (
        P("row", "col", None, None),
        P("row", "col"),
        P("row", "col"),
        P("row", "col"),
        P(),
        P(None, "row", None, None),
        P(),
        P(),
    )
    return jax.shard_map(
        per_device,
        mesh=mesh,
        in_specs=placed,
        out_specs=(P(None, "row", "col", None), P()),
        check_vma=False,
    )
```
